32 devices in a mesh: groups: 2 (over x), view: 16 (over z, y, core).
Axes of the slice: x: 2, y: 2, z: 4, core: 2. Of those that a mesh axis runs over, the one named last changes fastest.
Arguments:
- query_vectors: bfloat16 [32, 16, 8, 4096], P(('groups', 'view')), parts along dimension 0, may hold values from -6 to 6
- key_vectors: bfloat16 [32, 16, 8, 4096], P(('groups', 'view')), parts along dimension 0, may hold values from -6 to 6
- value_vectors: bfloat16 [32, 16, 8, 4096], P(('groups', 'view')), parts along dimension 0, may hold values from -6 to 6
- request_of_slot: int32 [8], P('groups'), parts along dimension 0, may hold values from 0 to 2, as said below
Outputs:
- attended: bfloat16 [32, 16, 8, 4096], P(('groups', 'view')), parts along dimension 0
The draws below stay inside these ranges and needn't reach their ends.
There are 2 independent parts, one for each index of `groups`. The reference program is written for one: setup_inputs(seed, part) draws one part's arguments, and reference() takes and returns one part's arrays. A program takes and returns all parts, laid end to end along the dimension named above; each array names one. Nothing has to cross between parts.
Inputs may be any that keep to these rules, and one draw needn't show every extreme that they name: `request_of_slot`: each request holds 1 to 2 slots, not necessarily consecutive, and one holds exactly 2.
All inputs are finite; a program needn't handle non-finite values.
Results may differ from the reference program's by a relative error of at most 0.0044.
Values may be sent and summed in bfloat16 or wider, within the bound.
No kernel may reach another device: no remote copies, remote signals or barrier semaphores. Data moves between devices by JAX's collectives and lax.ppermute only.
A program may use at most 64 MiB of HBM per device.

```python
import jax
import jax.numpy as jnp
from jax import lax

HEADS = 32
HS = 128
ROWS = 16
COLS = 8
VSLOTS = 4
IMAGES = 16
REQS = 3
MAXV = 2


def drawn_pair(key):
    full_shape = (IMAGES, ROWS, COLS, HEADS * HS)
    query_draw = jnp.clip(jax.random.normal(jax.random.fold_in(key, 701), full_shape, jnp.float32), -5.5, 5.5)
    key_draw = jnp.clip(jax.random.normal(jax.random.fold_in(key, 702), full_shape, jnp.float32), -5.5, 5.5)
    return (query_draw, key_draw)


def draw_query_vectors(key, part):
    return drawn_pair(key)[0].astype(jnp.bfloat16)


def draw_key_vectors(key, part):
    return drawn_pair(key)[1].astype(jnp.bfloat16)


def draw_request_of_slot(key, part):
    half_slots = VSLOTS // 2
    extras_count = VSLOTS - MAXV - REQS + 1
    extra_labels = jax.random.randint(jax.random.fold_in(key, 801), (extras_count,), 1, REQS).astype(jnp.int32)
    raw_labels = jnp.concatenate([jnp.zeros((MAXV,), jnp.int32), jnp.arange(1, REQS, dtype=jnp.int32), extra_labels])
    relabel = jax.random.permutation(jax.random.fold_in(key, 802), REQS).astype(jnp.int32)
    sequence = relabel[raw_labels]
    start_slot = jax.random.randint(jax.random.fold_in(key, 803), (), 0, half_slots).astype(jnp.int32)
    scores = jax.random.permutation(jax.random.fold_in(key, 804), VSLOTS).astype(jnp.int32)
    scores = scores.at[start_slot].set(-2).at[start_slot + half_slots].set(-1)
    placing = jnp.argsort(scores, stable=True).astype(jnp.int32)
    return jnp.zeros((VSLOTS,), jnp.int32).at[placing].set(sequence)


def shard_levels(key, shape, shards, least, top_value):
    loudness, own = 1.0, jax.random.fold_in(key, 6)
    for axis_at, shards_of in shards:
        draws = jnp.exp(jax.random.uniform(jax.random.fold_in(own, axis_at), (shards_of,), jnp.float32, least / len(shards), top_value / len(shards)))
        loudness = loudness * jnp.repeat(draws, shape[axis_at] // shards_of).reshape([-1 if axis == axis_at else 1 for axis in range(len(shape))])
    return loudness


def gaussian(stream_key, shape, scale, reach, shards=(), kind=jnp.bfloat16):
    gain = shard_levels(stream_key, shape, shards, -0.22, 0.18) if shards else 1.0
    array = jax.random.normal(stream_key, shape, jnp.float32) * scale * gain
    return jnp.minimum(jnp.maximum(array, -reach), reach).astype(kind)


def setup_inputs(seed: int = 0, part: int = 0) -> dict:
    arg_keys = jax.random.split(jax.random.key(seed), 5)
    part_keys = jax.random.split(jax.random.fold_in(arg_keys[4], part), 5)
    return {
        "query_vectors": draw_query_vectors(jax.random.fold_in(jax.random.fold_in(arg_keys[4], part), 71), part),
        "key_vectors": draw_key_vectors(jax.random.fold_in(jax.random.fold_in(arg_keys[4], part), 71), part),
        "value_vectors": gaussian(part_keys[2], (IMAGES, ROWS, COLS, HEADS * HS), 1.0, 6.0, ((0, 16),)),
        "request_of_slot": draw_request_of_slot(jax.random.fold_in(jax.random.fold_in(arg_keys[4], part), 71), part),
    }


NEG_FILL = -1.0e30


def partial_softmax(query_part, key_part, value_part, allowed):
    scaling = HS ** -0.5
    scores = jnp.einsum("nhx,khx->hnk", query_part.astype(jnp.float32), key_part.astype(jnp.float32)) * scaling
    scores = jnp.where(allowed[None], scores, NEG_FILL)
    maximum = jnp.max(scores, axis=2)
    raised = jnp.exp(scores - maximum[:, :, None])
    totals = jnp.sum(raised, axis=2)
    weights = lax.optimization_barrier(raised.astype(jnp.bfloat16))
    summed = jnp.einsum("hnk,khx->nhx", weights.astype(jnp.float32), value_part.astype(jnp.float32))
    return maximum.T, totals.T, summed


def combine(first_part, second_part):
    highest = jnp.maximum(first_part[0], second_part[0])
    first_scale = jnp.exp(first_part[0] - highest)
    second_scale = jnp.exp(second_part[0] - highest)
    denominator = first_part[1] * first_scale + second_part[1] * second_scale
    numerator = first_part[2] * first_scale[..., None] + second_part[2] * second_scale[..., None]
    return (numerator / denominator[..., None]).astype(jnp.bfloat16)


def reference(query_vectors, key_vectors, value_vectors, request_of_slot):
    pair_tokens = 2 * ROWS * COLS

    def by_slot(tensor):
        return tensor.reshape(2 * VSLOTS, pair_tokens, HEADS, HS)

    def by_row(tensor):
        shaped = tensor.reshape(VSLOTS, 2, 2, ROWS, COLS, HEADS, HS)
        return shaped.transpose(1, 3, 0, 2, 4, 5, 6).reshape(2 * ROWS, 2 * VSLOTS * COLS, HEADS, HS)

    def from_row(tensor):
        trailing = tensor.shape[2:]
        shaped = tensor.reshape((2, ROWS, VSLOTS, 2, COLS) + trailing)
        permuted = (2, 0, 3, 1, 4) + tuple(range(5, 5 + len(trailing)))
        return shaped.transpose(permuted).reshape((IMAGES, ROWS, COLS) + trailing)

    row_index = (jnp.arange(pair_tokens) // COLS) % ROWS
    local_allowed = row_index[:, None] != row_index[None, :]
    slot_request = jnp.broadcast_to(request_of_slot[:, None], (VSLOTS, 2 * COLS)).reshape(-1)
    row_allowed = slot_request[:, None] == slot_request[None, :]

    def local_step(triple):
        return partial_softmax(triple[0], triple[1], triple[2], local_allowed)

    def row_step(triple):
        return partial_softmax(triple[0], triple[1], triple[2], row_allowed)

    local_raw = lax.map(local_step, (by_slot(query_vectors), by_slot(key_vectors), by_slot(value_vectors)))
    local_part = tuple(part_item.reshape((IMAGES, ROWS, COLS) + part_item.shape[2:]) for part_item in local_raw)
    row_raw = lax.map(row_step, (by_row(query_vectors), by_row(key_vectors), by_row(value_vectors)))
    row_part = tuple(from_row(part_item) for part_item in row_raw)
    attended = combine(local_part, row_part)
    return attended.reshape(IMAGES, ROWS, COLS, HEADS * HS)
```

```python
import functools

import jax
import jax.numpy as jnp
from jax import lax
from jax.experimental import pallas as pl
from jax.experimental.pallas import tpu as pltpu
from jax.sharding import PartitionSpec as P

HEADS = 32
HS = 128
ROWS = 16
COLS = 8


NEG_FILL = -1e30


def partner(value, axis, distance):
    return lax.ppermute(value, axis, [(i, i ^ 1 << distance) for i in range(lax.axis_size(axis))])


def masked_softmax(scores, allowed):
    scores = jnp.where(allowed, scores, NEG_FILL)
    maximum = jnp.max(scores, axis=-1)
    raised = jnp.exp(scores - maximum[..., None])
    totals = jnp.sum(raised, axis=-1)
    return (maximum, totals, raised.astype(jnp.bfloat16))


def combine(first_part, second_part):
    highest = jnp.maximum(first_part[0], second_part[0])
    first_scale = jnp.exp(first_part[0] - highest)
    second_scale = jnp.exp(second_part[0] - highest)
    denominator = first_part[1] * first_scale + second_part[1] * second_scale
    numerator = first_part[2] * first_scale[..., None] + second_part[2] * second_scale[..., None]
    return (numerator / denominator[..., None]).astype(jnp.bfloat16)


def into_rows(tensor, row_blocks, head_groups):
    trailing = tensor.shape[3:]
    block_rows = tensor.shape[0] // row_blocks
    width_cols = tensor.shape[1]
    group_heads = tensor.shape[2] // head_groups
    shaped = tensor.reshape(
        (row_blocks, block_rows, width_cols, head_groups, group_heads) + trailing
    )
    permuted = (0, 3, 1, 2, 4) + tuple(range(5, 5 + len(trailing)))
    return shaped.transpose(permuted).reshape(
        (row_blocks * head_groups, block_rows, width_cols, group_heads) + trailing
    )


def into_tokens(tensor, row_blocks, head_groups):
    trailing = tensor.shape[4:]
    block_rows = tensor.shape[1]
    width_cols = tensor.shape[2]
    group_heads = tensor.shape[3]
    shaped = tensor.reshape(
        (row_blocks, head_groups, block_rows, width_cols, group_heads) + trailing
    )
    permuted = (0, 2, 3, 1, 4) + tuple(range(5, 5 + len(trailing)))
    return shaped.transpose(permuted).reshape(
        (row_blocks * block_rows * width_cols, head_groups * group_heads) + trailing
    )


def many_slots(query_vectors, key_vectors, value_vectors, request_of_slot):
    scaling = HS ** (-0.5)
    token_count = ROWS * COLS
    partner_key, partner_value = partner((key_vectors, value_vectors), "view", 0)
    head_blocks = 4
    block_heads = HEADS // head_blocks
    own_query = query_vectors.reshape(token_count, head_blocks, block_heads, HS)
    both_keys = jnp.concatenate(
        [
            key_vectors.reshape(token_count, head_blocks, block_heads, HS),
            partner_key.reshape(token_count, head_blocks, block_heads, HS),
        ],
        axis=0,
    )
    both_values = jnp.concatenate(
        [
            value_vectors.reshape(token_count, head_blocks, block_heads, HS),
            partner_value.reshape(token_count, head_blocks, block_heads, HS),
        ],
        axis=0,
    )
    query_row = jnp.arange(token_count) // COLS
    key_row = jnp.arange(2 * token_count) % token_count // COLS
    local_allowed = query_row[:, None] != key_row[None, :]

    def local_block(triple):
        block_scores = (
            jnp.einsum("nhx,khx->hnk", triple[0], triple[1], preferred_element_type=jnp.float32)
            * scaling
        )
        block_peak, block_total, block_weights = masked_softmax(block_scores, local_allowed[None])
        block_sum = jnp.einsum(
            "hnk,khx->nhx", block_weights, triple[2], preferred_element_type=jnp.float32
        )
        return (block_peak.T, block_total.T, block_sum)

    block_peaks, block_totals, block_sums = lax.map(
        local_block,
        (
            jnp.moveaxis(own_query, 1, 0),
            jnp.moveaxis(both_keys, 1, 0),
            jnp.moveaxis(both_values, 1, 0),
        ),
    )
    local_peak = jnp.moveaxis(block_peaks, 0, 1).reshape(token_count, HEADS)
    local_total = jnp.moveaxis(block_totals, 0, 1).reshape(token_count, HEADS)
    local_sum = jnp.moveaxis(block_sums, 0, 1).reshape(token_count, HEADS, HS)
    device_count = lax.axis_size("view")
    slot_count = device_count // 4
    pass_images = device_count // 2
    head_groups = 8
    row_blocks = device_count // head_groups
    block_rows = ROWS // row_blocks
    slot_request = jnp.broadcast_to(
        request_of_slot[:, None], (request_of_slot.shape[0], 2 * COLS)
    ).reshape(-1)
    row_allowed = slot_request[:, None] == slot_request[None, :]

    def arrange(tensor):
        shaped = tensor.reshape(slot_count, 2, 2, block_rows, COLS, HS).transpose(1, 3, 0, 2, 4, 5)
        return shaped.reshape(2 * block_rows, pass_images * COLS, HS)

    def restore(tensor):
        trailing = tensor.shape[2:]
        shaped = tensor.reshape((2, block_rows, slot_count, 2, COLS) + trailing)
        permuted = (2, 0, 3, 1, 4) + tuple(range(5, 5 + len(trailing)))
        return shaped.transpose(permuted).reshape((device_count, block_rows, COLS) + trailing)

    def one_head(triple):
        row_scores = (
            jnp.einsum(
                "bnx,bkx->bnk",
                arrange(triple[0]),
                arrange(triple[1]),
                preferred_element_type=jnp.float32,
            )
            * scaling
        )
        row_peak, row_total, row_weights = masked_softmax(row_scores, row_allowed[None])
        row_sum = jnp.einsum(
            "bnk,bkx->bnx", row_weights, arrange(triple[2]), preferred_element_type=jnp.float32
        )
        return (restore(row_peak), restore(row_total), restore(row_sum))

    query_rows = into_rows(query_vectors.reshape(ROWS, COLS, HEADS, HS), row_blocks, head_groups)
    key_rows = into_rows(key_vectors.reshape(ROWS, COLS, HEADS, HS), row_blocks, head_groups)
    value_rows = into_rows(value_vectors.reshape(ROWS, COLS, HEADS, HS), row_blocks, head_groups)
    by_head = (
        jnp.moveaxis(
            lax.all_to_all(query_rows, "view", split_axis=0, concat_axis=0, tiled=True), 3, 0
        ),
        jnp.moveaxis(
            lax.all_to_all(key_rows, "view", split_axis=0, concat_axis=0, tiled=True), 3, 0
        ),
        jnp.moveaxis(
            lax.all_to_all(value_rows, "view", split_axis=0, concat_axis=0, tiled=True), 3, 0
        ),
    )
    row_peaks, row_totals, row_sums = lax.map(one_head, by_head)
    peak_part = jnp.moveaxis(row_peaks, 0, 3)
    total_part = jnp.moveaxis(row_totals, 0, 3)
    sum_part = jnp.moveaxis(row_sums, 0, 3)
    row_peak = lax.all_to_all(peak_part, "view", split_axis=0, concat_axis=0, tiled=True)
    row_total = lax.all_to_all(total_part, "view", split_axis=0, concat_axis=0, tiled=True)
    row_sum = lax.all_to_all(sum_part, "view", split_axis=0, concat_axis=0, tiled=True)
    row_peak = into_tokens(row_peak, row_blocks, head_groups)
    row_total = into_tokens(row_total, row_blocks, head_groups)
    row_sum = into_tokens(row_sum, row_blocks, head_groups)
    attended = combine((local_peak, local_total, local_sum), (row_peak, row_total, row_sum))
    return attended.reshape(1, ROWS, COLS, HEADS * HS)


SCALING = HS ** (-0.5)
LANES = 128
PIECES = 3
CHUNKS = 2


def scores_of(query, keys):
    return lax.dot_general(query, keys, (((1,), (1,)), ((), ())), preferred_element_type=jnp.float32)


def own_kernel(query_ref, first_key, second_key, first_value, second_value, mean_ref, lse_ref):
    step = pl.program_id(0)
    block_heads = query_ref.shape[1] // HS
    lane = lax.broadcasted_iota(jnp.int32, lse_ref.shape, 1)

    @pl.when(step == 0)
    def _():
        lse_ref[...] = jnp.zeros_like(lse_ref)

    found = lse_ref[...]
    for head in range(block_heads):
        at = slice(head * HS, (head + 1) * HS)
        first = scores_of(query_ref[:, at], first_key[:, at])
        second = scores_of(query_ref[:, at], second_key[:, at])
        peak = jnp.max(jnp.maximum(first, second), axis=1, keepdims=True)
        first = jnp.exp((first - peak) * SCALING)
        second = jnp.exp((second - peak) * SCALING)
        total = jnp.sum(first + second, axis=1, keepdims=True)
        summed = jnp.dot(
            first.astype(jnp.bfloat16), first_value[:, at], preferred_element_type=jnp.float32
        ) + jnp.dot(
            second.astype(jnp.bfloat16), second_value[:, at], preferred_element_type=jnp.float32
        )
        mean_ref[:, at] = summed / total
        lse = peak * SCALING + jnp.log(total)
        found = jnp.where(lane == step * block_heads + head, lse, found)
    lse_ref[...] = found


def own_attention(query, keys, values, block_heads=2):
    tokens, width = query.shape
    heads = width // HS
    block = pl.BlockSpec((tokens, block_heads * HS), lambda i: (0, i))
    return pl.pallas_call(
        own_kernel,
        grid=(heads // block_heads,),
        in_specs=[block] * 5,
        out_specs=[block, pl.BlockSpec((tokens, LANES), lambda i: (0, 0))],
        out_shape=[
            jax.ShapeDtypeStruct((tokens, width), jnp.float32),
            jax.ShapeDtypeStruct((tokens, LANES), jnp.float32),
        ],
        cost_estimate=pl.CostEstimate(
            flops=8 * tokens * tokens * width, bytes_accessed=14 * tokens * width, transcendentals=0
        ),
        name="own_attention",
    )(query, *keys, *values)


def guest_kernel(query_ref, first_key, second_key, first_value, second_value, sent_ref):
    tokens, width = query_ref.shape
    query_row = lax.broadcasted_iota(jnp.int32, (tokens, tokens), 0) // COLS
    key_row = lax.broadcasted_iota(jnp.int32, (tokens, tokens), 1) // COLS
    same_row = query_row == key_row
    lane = lax.broadcasted_iota(jnp.int32, (tokens, LANES), 1)
    heads = width // HS

    def one_head(head, found):
        at = pl.ds(pl.multiple_of(head * HS, HS), HS)
        query = query_ref[:, at]
        first = jnp.where(same_row, scores_of(query, first_key[:, at]), NEG_FILL)
        second = jnp.where(same_row, scores_of(query, second_key[:, at]), NEG_FILL)
        peak = jnp.max(jnp.maximum(first, second), axis=1, keepdims=True)
        first = jnp.exp((first - peak) * SCALING)
        second = jnp.exp((second - peak) * SCALING)
        total = jnp.sum(first + second, axis=1, keepdims=True)
        summed = jnp.dot(
            first.astype(jnp.bfloat16), first_value[:, at], preferred_element_type=jnp.float32
        ) + jnp.dot(
            second.astype(jnp.bfloat16), second_value[:, at], preferred_element_type=jnp.float32
        )
        sent_ref[:, at] = (summed / total).astype(jnp.bfloat16)
        left = peak * SCALING + jnp.log(total)
        for piece in range(PIECES):
            part = left.astype(jnp.bfloat16).astype(jnp.float32)
            left = left - part
            found = jnp.where(lane == piece * heads + head, part, found)
        return found

    found = lax.fori_loop(0, heads, one_head, jnp.zeros((tokens, LANES), jnp.float32), unroll=2)
    sent_ref[:, width:] = found.astype(jnp.bfloat16)


def guest_attention(query, keys, values, chunk):
    tokens, width = query.shape
    whole = pl.BlockSpec((tokens, width), lambda i: (0, 0))
    block = pl.BlockSpec((tokens, width), lambda i: (chunk, 0))
    return pl.pallas_call(
        guest_kernel,
        grid=(1,),
        in_specs=[whole] + [block] * 4,
        out_specs=pl.BlockSpec((tokens, width + LANES), lambda i: (0, 0)),
        out_shape=jax.ShapeDtypeStruct((tokens, width + LANES), jnp.bfloat16),
        cost_estimate=pl.CostEstimate(
            flops=8 * tokens * tokens * width, bytes_accessed=12 * tokens * width, transcendentals=0
        ),
        name="guest_attention",
    )(query, *keys, *values)


def merge_kernel(has_guest, mean_ref, lse_ref, sent_ref, *rest):
    out_ref = rest[-1]
    width = mean_ref.shape[1]
    heads = width // HS
    pieces = sent_ref[:, width:].astype(jnp.float32)
    lse = pieces
    for piece in range(1, PIECES):
        lse = lse + pltpu.roll(pieces, LANES - piece * heads, 1)
    lse = jnp.where(has_guest[0] > 0, lse, NEG_FILL)
    share = 1.0 / (1.0 + jnp.exp(lse_ref[...] - lse))
    for head in range(heads):
        at = slice(head * HS, (head + 1) * HS)
        own = mean_ref[:, at]
        guest = sent_ref[:, at].astype(jnp.float32)
        out_ref[:, at] = (own + share[:, head : head + 1] * (guest - own)).astype(jnp.bfloat16)


def merge(has_guest, mean, lse, sent, chunk, before, steps=4):
    tokens, width = mean.shape
    part_tokens = sent.shape[0]
    block_tokens = part_tokens // steps
    here = lambda i, flag: (chunk * steps + i, 0)
    return pl.pallas_call(
        merge_kernel,
        grid_spec=pltpu.PrefetchScalarGridSpec(
            num_scalar_prefetch=1,
            grid=(steps,),
            in_specs=[
                pl.BlockSpec((block_tokens, width), here),
                pl.BlockSpec((block_tokens, LANES), here),
                pl.BlockSpec((block_tokens, width + LANES), lambda i, flag: (i, 0)),
            ]
            + [pl.BlockSpec(memory_space=pl.ANY)] * len(before),
            out_specs=pl.BlockSpec((block_tokens, width), here),
        ),
        out_shape=jax.ShapeDtypeStruct((tokens, width), jnp.bfloat16),
        input_output_aliases={4: 0} if before else {},
        cost_estimate=pl.CostEstimate(
            flops=4 * part_tokens * width, bytes_accessed=8 * part_tokens * width, transcendentals=0
        ),
        name="merge",
    )(has_guest, mean, lse, sent, *before)


def matchings(slots):
    if len(slots) < 2:
        return [[]]
    first, rest = slots[0], slots[1:]
    found = list(matchings(rest))
    for other in rest:
        left = [slot for slot in rest if slot != other]
        found += [[(first, other)] + more for more in matchings(left)]
    return found


def device_pairs(matching, slot_devices):
    ways = [way for pair in matching for way in (pair, pair[::-1])]
    return [
        (source * slot_devices + inner, target * slot_devices + inner)
        for source, target in ways
        for inner in range(slot_devices)
    ]


def few_slots(query_vectors, key_vectors, value_vectors, request_of_slot):
    device_count = lax.axis_size("view")
    slot_count = request_of_slot.shape[0]
    slot_devices = device_count // slot_count
    token_count = ROWS * COLS
    width = HEADS * HS
    chunk_tokens = token_count // CHUNKS
    query = query_vectors.reshape(token_count, width)
    key = key_vectors.reshape(token_count, width)
    value = value_vectors.reshape(token_count, width)
    query_parts = [
        lax.slice_in_dim(query, part * chunk_tokens, (part + 1) * chunk_tokens)
        for part in range(CHUNKS)
    ]
    requests = [request_of_slot[slot] for slot in range(slot_count)]
    every = [matching for matching in matchings(list(range(slot_count))) if matching]
    branch = jnp.int32(0)
    for number, matching in enumerate(every):
        fits = functools.reduce(
            jnp.logical_and, [requests[one] == requests[other] for one, other in matching]
        )
        branch = jnp.where(fits, jnp.int32(number), branch)
    my_slot = lax.axis_index("view") // slot_devices

    def exchange(matching):
        pairs = device_pairs(matching, slot_devices)
        members = [slot for pair in matching for slot in pair]

        def run(key, value, query, *parts):
            guests = [lax.ppermute(part, "view", pairs) for part in parts]
            keys = (key, partner(key, "view", 0))
            values = (value, partner(value, "view", 0))
            mean, lse = own_attention(query, keys, values)
            backs = [
                lax.ppermute(guest_attention(guest, keys, values, part), "view", pairs)
                for part, guest in enumerate(guests)
            ]
            has_guest = functools.reduce(jnp.logical_or, [my_slot == slot for slot in members])
            has_guest = has_guest.astype(jnp.int32).reshape(1)
            out = ()
            for part, back in enumerate(backs):
                out = (merge(has_guest, mean, lse, back, part, out),)
            return out[0]

        return run

    attended = lax.switch(branch, [exchange(matching) for matching in every], key, value, query, *query_parts)
    return attended.reshape(1, ROWS, COLS, HEADS * HS)


def shards(query_vectors, key_vectors, value_vectors, request_of_slot):
    most_views = request_of_slot.shape[0] // 2
    path = few_slots if most_views == 2 else many_slots
    return path(query_vectors, key_vectors, value_vectors, request_of_slot)


def solution(mesh):
    return jax.shard_map(
        shards,
        mesh=mesh,
        in_specs=(
            P(("groups", "view"), None, None, None),
            P(("groups", "view"), None, None, None),
            P(("groups", "view"), None, None, None),
            P("groups"),
        ),
        out_specs=P(("groups", "view"), None, None, None),
        check_vma=False,
    )
```

```python
import functools

import jax
import jax.numpy as jnp
from jax import lax
from jax.experimental import pallas as pl
from jax.experimental.pallas import tpu as pltpu
from jax.sharding import PartitionSpec as P

HEADS = 32
HS = 128
ROWS = 16
COLS = 8


NEG_FILL = -1e30


def partner(value, axis, distance):
    return lax.ppermute(value, axis, [(i, i ^ 1 << distance) for i in range(lax.axis_size(axis))])


def masked_softmax(scores, allowed):
    scores = jnp.where(allowed, scores, NEG_FILL)
    maximum = jnp.max(scores, axis=-1)
    raised = jnp.exp(scores - maximum[..., None])
    totals = jnp.sum(raised, axis=-1)
    return (maximum, totals, raised.astype(jnp.bfloat16))


def combine(first_part, second_part):
    highest = jnp.maximum(first_part[0], second_part[0])
    first_scale = jnp.exp(first_part[0] - highest)
    second_scale = jnp.exp(second_part[0] - highest)
    denominator = first_part[1] * first_scale + second_part[1] * second_scale
    numerator = first_part[2] * first_scale[..., None] + second_part[2] * second_scale[..., None]
    return (numerator / denominator[..., None]).astype(jnp.bfloat16)


def into_rows(tensor, row_blocks, head_groups):
    trailing = tensor.shape[3:]
    block_rows = tensor.shape[0] // row_blocks
    width_cols = tensor.shape[1]
    group_heads = tensor.shape[2] // head_groups
    shaped = tensor.reshape(
        (row_blocks, block_rows, width_cols, head_groups, group_heads) + trailing
    )
    permuted = (0, 3, 1, 2, 4) + tuple(range(5, 5 + len(trailing)))
    return shaped.transpose(permuted).reshape(
        (row_blocks * head_groups, block_rows, width_cols, group_heads) + trailing
    )


def into_tokens(tensor, row_blocks, head_groups):
    trailing = tensor.shape[4:]
    block_rows = tensor.shape[1]
    width_cols = tensor.shape[2]
    group_heads = tensor.shape[3]
    shaped = tensor.reshape(
        (row_blocks, head_groups, block_rows, width_cols, group_heads) + trailing
    )
    permuted = (0, 2, 3, 1, 4) + tuple(range(5, 5 + len(trailing)))
    return shaped.transpose(permuted).reshape(
        (row_blocks * block_rows * width_cols, head_groups * group_heads) + trailing
    )


def many_slots(query_vectors, key_vectors, value_vectors, request_of_slot):
    scaling = HS ** (-0.5)
    token_count = ROWS * COLS
    partner_key, partner_value = partner((key_vectors, value_vectors), "view", 0)
    head_blocks = 4
    block_heads = HEADS // head_blocks
    own_query = query_vectors.reshape(token_count, head_blocks, block_heads, HS)
    both_keys = jnp.concatenate(
        [
            key_vectors.reshape(token_count, head_blocks, block_heads, HS),
            partner_key.reshape(token_count, head_blocks, block_heads, HS),
        ],
        axis=0,
    )
    both_values = jnp.concatenate(
        [
            value_vectors.reshape(token_count, head_blocks, block_heads, HS),
            partner_value.reshape(token_count, head_blocks, block_heads, HS),
        ],
        axis=0,
    )
    query_row = jnp.arange(token_count) // COLS
    key_row = jnp.arange(2 * token_count) % token_count // COLS
    local_allowed = query_row[:, None] != key_row[None, :]

    def local_block(triple):
        block_scores = (
            jnp.einsum("nhx,khx->hnk", triple[0], triple[1], preferred_element_type=jnp.float32)
            * scaling
        )
        block_peak, block_total, block_weights = masked_softmax(block_scores, local_allowed[None])
        block_sum = jnp.einsum(
            "hnk,khx->nhx", block_weights, triple[2], preferred_element_type=jnp.float32
        )
        return (block_peak.T, block_total.T, block_sum)

    block_peaks, block_totals, block_sums = lax.map(
        local_block,
        (
            jnp.moveaxis(own_query, 1, 0),
            jnp.moveaxis(both_keys, 1, 0),
            jnp.moveaxis(both_values, 1, 0),
        ),
    )
    local_peak = jnp.moveaxis(block_peaks, 0, 1).reshape(token_count, HEADS)
    local_total = jnp.moveaxis(block_totals, 0, 1).reshape(token_count, HEADS)
    local_sum = jnp.moveaxis(block_sums, 0, 1).reshape(token_count, HEADS, HS)
    device_count = lax.axis_size("view")
    slot_count = device_count // 4
    pass_images = device_count // 2
    head_groups = 8
    row_blocks = device_count // head_groups
    block_rows = ROWS // row_blocks
    slot_request = jnp.broadcast_to(
        request_of_slot[:, None], (request_of_slot.shape[0], 2 * COLS)
    ).reshape(-1)
    row_allowed = slot_request[:, None] == slot_request[None, :]

    def arrange(tensor):
        shaped = tensor.reshape(slot_count, 2, 2, block_rows, COLS, HS).transpose(1, 3, 0, 2, 4, 5)
        return shaped.reshape(2 * block_rows, pass_images * COLS, HS)

    def restore(tensor):
        trailing = tensor.shape[2:]
        shaped = tensor.reshape((2, block_rows, slot_count, 2, COLS) + trailing)
        permuted = (2, 0, 3, 1, 4) + tuple(range(5, 5 + len(trailing)))
        return shaped.transpose(permuted).reshape((device_count, block_rows, COLS) + trailing)

    def one_head(triple):
        row_scores = (
            jnp.einsum(
                "bnx,bkx->bnk",
                arrange(triple[0]),
                arrange(triple[1]),
                preferred_element_type=jnp.float32,
            )
            * scaling
        )
        row_peak, row_total, row_weights = masked_softmax(row_scores, row_allowed[None])
        row_sum = jnp.einsum(
            "bnk,bkx->bnx", row_weights, arrange(triple[2]), preferred_element_type=jnp.float32
        )
        return (restore(row_peak), restore(row_total), restore(row_sum))

    query_rows = into_rows(query_vectors.reshape(ROWS, COLS, HEADS, HS), row_blocks, head_groups)
    key_rows = into_rows(key_vectors.reshape(ROWS, COLS, HEADS, HS), row_blocks, head_groups)
    value_rows = into_rows(value_vectors.reshape(ROWS, COLS, HEADS, HS), row_blocks, head_groups)
    by_head = (
        jnp.moveaxis(
            lax.all_to_all(query_rows, "view", split_axis=0, concat_axis=0, tiled=True), 3, 0
        ),
        jnp.moveaxis(
            lax.all_to_all(key_rows, "view", split_axis=0, concat_axis=0, tiled=True), 3, 0
        ),
        jnp.moveaxis(
            lax.all_to_all(value_rows, "view", split_axis=0, concat_axis=0, tiled=True), 3, 0
        ),
    )
    row_peaks, row_totals, row_sums = lax.map(one_head, by_head)
    peak_part = jnp.moveaxis(row_peaks, 0, 3)
    total_part = jnp.moveaxis(row_totals, 0, 3)
    sum_part = jnp.moveaxis(row_sums, 0, 3)
    row_peak = lax.all_to_all(peak_part, "view", split_axis=0, concat_axis=0, tiled=True)
    row_total = lax.all_to_all(total_part, "view", split_axis=0, concat_axis=0, tiled=True)
    row_sum = lax.all_to_all(sum_part, "view", split_axis=0, concat_axis=0, tiled=True)
    row_peak = into_tokens(row_peak, row_blocks, head_groups)
    row_total = into_tokens(row_total, row_blocks, head_groups)
    row_sum = into_tokens(row_sum, row_blocks, head_groups)
    attended = combine((local_peak, local_total, local_sum), (row_peak, row_total, row_sum))
    return attended.reshape(1, ROWS, COLS, HEADS * HS)


SCALING = HS ** (-0.5)
LANES = 128
PIECES = 3
CHUNKS = 2
GROUP = 8


def scores_of(query, keys):
    return lax.dot_general(query, keys, (((1,), (1,)), ((), ())), preferred_element_type=jnp.float32)


def lanes_of(head):
    return pl.ds(pl.multiple_of(head * HS, HS), HS)


def partial_softmax(heads, query_ref, key_refs, value_refs, allowed):
    scores = []
    for head in heads:
        at = lanes_of(head)
        keys = jnp.concatenate([ref[:, at] for ref in key_refs], axis=0)
        scores.append(scores_of(query_ref[:, at], keys))
    if allowed is not None:
        scores = [jnp.where(allowed, score, NEG_FILL) for score in scores]
    peaks = [jnp.max(score, axis=1, keepdims=True) for score in scores]
    weights = [
        jnp.exp((score - peak) * SCALING).astype(jnp.bfloat16)
        for score, peak in zip(scores, peaks)
    ]
    results = []
    for head, peak, weight in zip(heads, peaks, weights):
        at = lanes_of(head)
        values = jnp.concatenate([ref[:, at] for ref in value_refs], axis=0)
        ones = jnp.ones_like(values)
        both = jnp.dot(
            weight, jnp.concatenate([values, ones], axis=1), preferred_element_type=jnp.float32
        )
        total = both[:, HS:]
        results.append((both[:, :HS] / total, peak * SCALING + jnp.log(total)))
    return results


def own_kernel(query_ref, first_key, second_key, first_value, second_value, mean_ref, lse_ref):
    heads = query_ref.shape[1] // HS
    lane = lax.broadcasted_iota(jnp.int32, lse_ref.shape, 1)

    def one_group(group, found):
        numbers = [group * GROUP + inner for inner in range(GROUP)]
        results = partial_softmax(
            numbers, query_ref, (first_key, second_key), (first_value, second_value), None
        )
        for head, (mean, lse) in zip(numbers, results):
            mean_ref[:, lanes_of(head)] = mean
            found = jnp.where(lane == head, lse, found)
        return found

    zeros = jnp.zeros(lse_ref.shape, jnp.float32)
    lse_ref[...] = lax.fori_loop(0, heads // GROUP, one_group, zeros)


def own_attention(query, keys, values):
    tokens, width = query.shape
    return pl.pallas_call(
        own_kernel,
        out_shape=[
            jax.ShapeDtypeStruct((tokens, width), jnp.float32),
            jax.ShapeDtypeStruct((tokens, LANES), jnp.float32),
        ],
        compiler_params=pltpu.CompilerParams(vmem_limit_bytes=24 * 2**20),
        cost_estimate=pl.CostEstimate(
            flops=8 * tokens * tokens * width, bytes_accessed=14 * tokens * width, transcendentals=0
        ),
        name="own_attention",
    )(query, *keys, *values)


def guest_kernel(query_ref, first_key, second_key, first_value, second_value, _, sent_ref):
    tokens, width = query_ref.shape
    shape = (tokens, 2 * tokens)
    query_row = lax.broadcasted_iota(jnp.int32, shape, 0) // COLS
    key_row = lax.broadcasted_iota(jnp.int32, shape, 1) % tokens // COLS
    same_row = query_row == key_row
    lane = lax.broadcasted_iota(jnp.int32, (tokens, LANES), 1)
    heads = width // HS

    def one_group(group, found):
        numbers = [group * GROUP + inner for inner in range(GROUP)]
        results = partial_softmax(
            numbers, query_ref, (first_key, second_key), (first_value, second_value), same_row
        )
        for head, (mean, lse) in zip(numbers, results):
            sent_ref[:, lanes_of(head)] = mean.astype(jnp.bfloat16)
            found = jnp.where(lane % heads == head, lse, found)
        return found

    left = lax.fori_loop(0, heads // GROUP, one_group, jnp.zeros((tokens, LANES), jnp.float32))
    packed = jnp.zeros((tokens, LANES), jnp.bfloat16)
    for piece in range(PIECES):
        part = left.astype(jnp.bfloat16)
        left = left - part.astype(jnp.float32)
        packed = jnp.where(lane // heads == piece, part.astype(jnp.float32), packed.astype(jnp.float32)).astype(jnp.bfloat16)
    sent_ref[:, width:] = packed


def guest_attention(query, keys, values, chunk, after):
    tokens, width = query.shape
    whole = pl.BlockSpec((tokens, width), lambda i: (0, 0))
    block = pl.BlockSpec((tokens, width), lambda i: (chunk, 0))
    return pl.pallas_call(
        guest_kernel,
        grid=(1,),
        in_specs=[whole] + [block] * 4 + [pl.BlockSpec(memory_space=pl.ANY)],
        out_specs=pl.BlockSpec((tokens, width + LANES), lambda i: (0, 0)),
        out_shape=jax.ShapeDtypeStruct((tokens, width + LANES), jnp.bfloat16),
        compiler_params=pltpu.CompilerParams(vmem_limit_bytes=24 * 2**20),
        cost_estimate=pl.CostEstimate(
            flops=8 * tokens * tokens * width, bytes_accessed=12 * tokens * width, transcendentals=0
        ),
        name="guest_attention",
    )(query, *keys, *values, after)


def merge_kernel(has_guest, mean_ref, lse_ref, sent_ref, *rest):
    out_ref = rest[-1]
    tokens, width = mean_ref.shape
    heads = width // HS
    pieces = sent_ref[:, width:].astype(jnp.float32)
    lse = pieces
    for piece in range(1, PIECES):
        lse = lse + pltpu.roll(pieces, LANES - piece * heads, 1)
    lse = jnp.where(has_guest[0] > 0, lse, NEG_FILL)
    share = 1.0 / (1.0 + jnp.exp(lse_ref[...] - lse))

    def one_group(group, share):
        for inner in range(GROUP):
            at = lanes_of(group * GROUP + inner)
            own = mean_ref[:, at]
            guest = sent_ref[:, at].astype(jnp.float32)
            out_ref[:, at] = (own + share[:, inner : inner + 1] * (guest - own)).astype(jnp.bfloat16)
        return pltpu.roll(share, LANES - GROUP, 1)

    lax.fori_loop(0, heads // GROUP, one_group, share)


def merge(has_guest, mean, lse, sent, chunk, before):
    tokens, width = mean.shape
    part_tokens = sent.shape[0]
    here = lambda i, flag: (chunk, 0)
    return pl.pallas_call(
        merge_kernel,
        grid_spec=pltpu.PrefetchScalarGridSpec(
            num_scalar_prefetch=1,
            grid=(1,),
            in_specs=[
                pl.BlockSpec((part_tokens, width), here),
                pl.BlockSpec((part_tokens, LANES), here),
                pl.BlockSpec((part_tokens, width + LANES), lambda i, flag: (0, 0)),
            ]
            + [pl.BlockSpec(memory_space=pl.ANY)] * len(before),
            out_specs=pl.BlockSpec((part_tokens, width), here),
        ),
        out_shape=jax.ShapeDtypeStruct((tokens, width), jnp.bfloat16),
        input_output_aliases={4: 0} if before else {},
        compiler_params=pltpu.CompilerParams(vmem_limit_bytes=16 * 2**20),
        cost_estimate=pl.CostEstimate(
            flops=4 * part_tokens * width, bytes_accessed=8 * part_tokens * width, transcendentals=0
        ),
        name="merge",
    )(has_guest, mean, lse, sent, *before)


def matchings(slots):
    if len(slots) < 2:
        return [[]]
    first, rest = slots[0], slots[1:]
    found = list(matchings(rest))
    for other in rest:
        left = [slot for slot in rest if slot != other]
        found += [[(first, other)] + more for more in matchings(left)]
    return found


def device_pairs(matching, slot_devices):
    ways = [way for pair in matching for way in (pair, pair[::-1])]
    return [
        (source * slot_devices + inner, target * slot_devices + inner)
        for source, target in ways
        for inner in range(slot_devices)
    ]


def which_matching(request_of_slot, every):
    def kernel(request_ref, number_ref):
        chosen = jnp.int32(0)
        for number, matching in enumerate(every):
            fits = functools.reduce(
                jnp.logical_and, [request_ref[one] == request_ref[other] for one, other in matching]
            )
            chosen = jnp.where(fits, jnp.int32(number), chosen)
        number_ref[0] = chosen

    return pl.pallas_call(
        kernel,
        in_specs=[pl.BlockSpec(memory_space=pltpu.SMEM)],
        out_specs=pl.BlockSpec(memory_space=pltpu.SMEM),
        out_shape=jax.ShapeDtypeStruct((1,), jnp.int32),
        name="which_matching",
    )(request_of_slot)[0]


def few_slots(query_vectors, key_vectors, value_vectors, request_of_slot):
    device_count = lax.axis_size("view")
    slot_count = request_of_slot.shape[0]
    slot_devices = device_count // slot_count
    token_count = ROWS * COLS
    width = HEADS * HS
    chunk_tokens = token_count // CHUNKS
    query = query_vectors.reshape(token_count, width)
    key = key_vectors.reshape(token_count, width)
    value = value_vectors.reshape(token_count, width)
    every = [matching for matching in matchings(list(range(slot_count))) if matching]
    branch = which_matching(request_of_slot, every)
    my_slot = lax.axis_index("view") // slot_devices

    def exchange(matching):
        pairs = device_pairs(matching, slot_devices)
        members = [slot for pair in matching for slot in pair]

        def run(key, value, query):
            guests, source = [], query
            for part in range(CHUNKS):
                sent = lax.slice_in_dim(source, part * chunk_tokens, (part + 1) * chunk_tokens)
                source, sent = lax.optimization_barrier((source, sent))
                guests.append(lax.ppermute(sent, "view", pairs))
            keys = (key, partner(key, "view", 0))
            values = (value, partner(value, "view", 0))
            mean, lse = own_attention(query, keys, values)
            backs = [
                lax.ppermute(guest_attention(guest, keys, values, part, lse), "view", pairs)
                for part, guest in enumerate(guests)
            ]
            has_guest = functools.reduce(jnp.logical_or, [my_slot == slot for slot in members])
            has_guest = has_guest.astype(jnp.int32).reshape(1)
            out = ()
            for part, back in enumerate(backs):
                out = (merge(has_guest, mean, lse, back, part, out),)
            return out[0]

        return run

    attended = lax.switch(branch, [exchange(matching) for matching in every], key, value, query)
    return attended.reshape(1, ROWS, COLS, HEADS * HS)


def shards(query_vectors, key_vectors, value_vectors, request_of_slot):
    most_views = request_of_slot.shape[0] // 2
    path = few_slots if most_views == 2 else many_slots
    return path(query_vectors, key_vectors, value_vectors, request_of_slot)


def solution(mesh):
    return jax.shard_map(
        shards,
        mesh=mesh,
        in_specs=(
            P(("groups", "view"), None, None, None),
            P(("groups", "view"), None, None, None),
            P(("groups", "view"), None, None, None),
            P("groups"),
        ),
        out_specs=P(("groups", "view"), None, None, None),
        check_vma=False,
    )
```

```python
import functools

import jax
import jax.numpy as jnp
from jax import lax
from jax.experimental import pallas as pl
from jax.experimental.pallas import tpu as pltpu
from jax.sharding import PartitionSpec as P


HEADS = 32
HS = 128
ROWS = 16
COLS = 8


NEG_FILL = -1e30


def partner(value, axis, distance):
    return lax.ppermute(value, axis, [(i, i ^ 1 << distance) for i in range(lax.axis_size(axis))])


def masked_softmax(scores, allowed):
    scores = jnp.where(allowed, scores, NEG_FILL)
    maximum = jnp.max(scores, axis=-1)
    raised = jnp.exp(scores - maximum[..., None])
    totals = jnp.sum(raised, axis=-1)
    return (maximum, totals, raised.astype(jnp.bfloat16))


def combine(first_part, second_part):
    highest = jnp.maximum(first_part[0], second_part[0])
    first_scale = jnp.exp(first_part[0] - highest)
    second_scale = jnp.exp(second_part[0] - highest)
    denominator = first_part[1] * first_scale + second_part[1] * second_scale
    numerator = first_part[2] * first_scale[..., None] + second_part[2] * second_scale[..., None]
    return (numerator / denominator[..., None]).astype(jnp.bfloat16)


def into_rows(tensor, row_blocks, head_groups):
    trailing = tensor.shape[3:]
    block_rows = tensor.shape[0] // row_blocks
    width_cols = tensor.shape[1]
    group_heads = tensor.shape[2] // head_groups
    shaped = tensor.reshape(
        (row_blocks, block_rows, width_cols, head_groups, group_heads) + trailing
    )
    permuted = (0, 3, 1, 2, 4) + tuple(range(5, 5 + len(trailing)))
    return shaped.transpose(permuted).reshape(
        (row_blocks * head_groups, block_rows, width_cols, group_heads) + trailing
    )


def into_tokens(tensor, row_blocks, head_groups):
    trailing = tensor.shape[4:]
    block_rows = tensor.shape[1]
    width_cols = tensor.shape[2]
    group_heads = tensor.shape[3]
    shaped = tensor.reshape(
        (row_blocks, head_groups, block_rows, width_cols, group_heads) + trailing
    )
    permuted = (0, 2, 3, 1, 4) + tuple(range(5, 5 + len(trailing)))
    return shaped.transpose(permuted).reshape(
        (row_blocks * block_rows * width_cols, head_groups * group_heads) + trailing
    )


def many_slots(query_vectors, key_vectors, value_vectors, request_of_slot):
    scaling = HS ** (-0.5)
    token_count = ROWS * COLS
    partner_key, partner_value = partner((key_vectors, value_vectors), "view", 0)
    head_blocks = 4
    block_heads = HEADS // head_blocks
    own_query = query_vectors.reshape(token_count, head_blocks, block_heads, HS)
    both_keys = jnp.concatenate(
        [
            key_vectors.reshape(token_count, head_blocks, block_heads, HS),
            partner_key.reshape(token_count, head_blocks, block_heads, HS),
        ],
        axis=0,
    )
    both_values = jnp.concatenate(
        [
            value_vectors.reshape(token_count, head_blocks, block_heads, HS),
            partner_value.reshape(token_count, head_blocks, block_heads, HS),
        ],
        axis=0,
    )
    query_row = jnp.arange(token_count) // COLS
    key_row = jnp.arange(2 * token_count) % token_count // COLS
    local_allowed = query_row[:, None] != key_row[None, :]

    def local_block(triple):
        block_scores = (
            jnp.einsum("nhx,khx->hnk", triple[0], triple[1], preferred_element_type=jnp.float32)
            * scaling
        )
        block_peak, block_total, block_weights = masked_softmax(block_scores, local_allowed[None])
        block_sum = jnp.einsum(
            "hnk,khx->nhx", block_weights, triple[2], preferred_element_type=jnp.float32
        )
        return (block_peak.T, block_total.T, block_sum)

    block_peaks, block_totals, block_sums = lax.map(
        local_block,
        (
            jnp.moveaxis(own_query, 1, 0),
            jnp.moveaxis(both_keys, 1, 0),
            jnp.moveaxis(both_values, 1, 0),
        ),
    )
    local_peak = jnp.moveaxis(block_peaks, 0, 1).reshape(token_count, HEADS)
    local_total = jnp.moveaxis(block_totals, 0, 1).reshape(token_count, HEADS)
    local_sum = jnp.moveaxis(block_sums, 0, 1).reshape(token_count, HEADS, HS)
    device_count = lax.axis_size("view")
    slot_count = device_count // 4
    pass_images = device_count // 2
    head_groups = 8
    row_blocks = device_count // head_groups
    block_rows = ROWS // row_blocks
    slot_request = jnp.broadcast_to(
        request_of_slot[:, None], (request_of_slot.shape[0], 2 * COLS)
    ).reshape(-1)
    row_allowed = slot_request[:, None] == slot_request[None, :]

    def arrange(tensor):
        shaped = tensor.reshape(slot_count, 2, 2, block_rows, COLS, HS).transpose(1, 3, 0, 2, 4, 5)
        return shaped.reshape(2 * block_rows, pass_images * COLS, HS)

    def restore(tensor):
        trailing = tensor.shape[2:]
        shaped = tensor.reshape((2, block_rows, slot_count, 2, COLS) + trailing)
        permuted = (2, 0, 3, 1, 4) + tuple(range(5, 5 + len(trailing)))
        return shaped.transpose(permuted).reshape((device_count, block_rows, COLS) + trailing)

    def one_head(triple):
        row_scores = (
            jnp.einsum(
                "bnx,bkx->bnk",
                arrange(triple[0]),
                arrange(triple[1]),
                preferred_element_type=jnp.float32,
            )
            * scaling
        )
        row_peak, row_total, row_weights = masked_softmax(row_scores, row_allowed[None])
        row_sum = jnp.einsum(
            "bnk,bkx->bnx", row_weights, arrange(triple[2]), preferred_element_type=jnp.float32
        )
        return (restore(row_peak), restore(row_total), restore(row_sum))

    query_rows = into_rows(query_vectors.reshape(ROWS, COLS, HEADS, HS), row_blocks, head_groups)
    key_rows = into_rows(key_vectors.reshape(ROWS, COLS, HEADS, HS), row_blocks, head_groups)
    value_rows = into_rows(value_vectors.reshape(ROWS, COLS, HEADS, HS), row_blocks, head_groups)
    by_head = (
        jnp.moveaxis(
            lax.all_to_all(query_rows, "view", split_axis=0, concat_axis=0, tiled=True), 3, 0
        ),
        jnp.moveaxis(
            lax.all_to_all(key_rows, "view", split_axis=0, concat_axis=0, tiled=True), 3, 0
        ),
        jnp.moveaxis(
            lax.all_to_all(value_rows, "view", split_axis=0, concat_axis=0, tiled=True), 3, 0
        ),
    )
    row_peaks, row_totals, row_sums = lax.map(one_head, by_head)
    peak_part = jnp.moveaxis(row_peaks, 0, 3)
    total_part = jnp.moveaxis(row_totals, 0, 3)
    sum_part = jnp.moveaxis(row_sums, 0, 3)
    row_peak = lax.all_to_all(peak_part, "view", split_axis=0, concat_axis=0, tiled=True)
    row_total = lax.all_to_all(total_part, "view", split_axis=0, concat_axis=0, tiled=True)
    row_sum = lax.all_to_all(sum_part, "view", split_axis=0, concat_axis=0, tiled=True)
    row_peak = into_tokens(row_peak, row_blocks, head_groups)
    row_total = into_tokens(row_total, row_blocks, head_groups)
    row_sum = into_tokens(row_sum, row_blocks, head_groups)
    attended = combine((local_peak, local_total, local_sum), (row_peak, row_total, row_sum))
    return attended.reshape(1, ROWS, COLS, HEADS * HS)


SCALING = HS ** (-0.5)
LANES = 128
PIECES = 3
GROUP = 8
QUERY_ROWS = (8, 8)
RETURN_ROWS = ((8,), (6, 2))
IN_VMEM = pl.BlockSpec(memory_space=pltpu.VMEM)
IN_PLACE = pl.BlockSpec(memory_space=pl.ANY)


def scores_of(query, keys):
    return lax.dot_general(query, keys, (((1,), (1,)), ((), ())), preferred_element_type=jnp.float32)


def lanes_of(head):
    return pl.ds(pl.multiple_of(head * HS, HS), HS)


def partial_softmax(heads, query_ref, key_refs, value_refs, rows, allowed):
    scores = []
    for head in heads:
        at = lanes_of(head)
        keys = jnp.concatenate([ref[rows, at] for ref in key_refs], axis=0)
        scores.append(scores_of(query_ref[:, at], keys))
    if allowed is not None:
        scores = [jnp.where(allowed, score, NEG_FILL) for score in scores]
    peaks = [jnp.max(score, axis=1, keepdims=True) for score in scores]
    weights = [
        jnp.exp((score - peak) * SCALING).astype(jnp.bfloat16)
        for score, peak in zip(scores, peaks)
    ]
    results = []
    for head, peak, weight in zip(heads, peaks, weights):
        at = lanes_of(head)
        values = jnp.concatenate([ref[rows, at] for ref in value_refs], axis=0)
        ones = jnp.ones_like(values)
        both = jnp.dot(
            weight, jnp.concatenate([values, ones], axis=1), preferred_element_type=jnp.float32
        )
        total = both[:, HS:]
        results.append((both[:, :HS] / total, peak * SCALING + jnp.log(total)))
    return results


def own_kernel(query_ref, first_key, second_key, first_value, second_value, mean_ref, lse_ref):
    heads = query_ref.shape[1] // HS
    lane = lax.broadcasted_iota(jnp.int32, lse_ref.shape, 1)

    def one_group(group, found):
        numbers = [group * GROUP + inner for inner in range(GROUP)]
        results = partial_softmax(
            numbers, query_ref, (first_key, second_key), (first_value, second_value), slice(None), None
        )
        for head, (mean, lse) in zip(numbers, results):
            mean_ref[:, lanes_of(head)] = mean
            found = jnp.where(lane == head, lse, found)
        return found

    zeros = jnp.zeros(lse_ref.shape, jnp.float32)
    lse_ref[...] = lax.fori_loop(0, heads // GROUP, one_group, zeros)


def own_attention(query, keys, values):
    tokens, width = query.shape
    return pl.pallas_call(
        own_kernel,
        out_shape=[
            jax.ShapeDtypeStruct((tokens, width), jnp.float32),
            jax.ShapeDtypeStruct((tokens, LANES), jnp.float32),
        ],
        compiler_params=pltpu.CompilerParams(vmem_limit_bytes=24 * 2**20),
        cost_estimate=pl.CostEstimate(
            flops=8 * tokens * tokens * width, bytes_accessed=14 * tokens * width, transcendentals=0
        ),
        name="own_attention",
    )(query, *keys, *values)


def guest_kernel(start, query_ref, first_key, second_key, first_value, second_value, _, *sent_refs):
    tokens, width = query_ref.shape
    rows = slice(start, start + tokens)
    shape = (tokens, 2 * tokens)
    query_row = lax.broadcasted_iota(jnp.int32, shape, 0) // COLS
    key_row = lax.broadcasted_iota(jnp.int32, shape, 1) % tokens // COLS
    same_row = query_row == key_row
    lane = lax.broadcasted_iota(jnp.int32, (tokens, LANES), 1)
    heads = width // HS

    def store(at, value):
        start = 0
        for sent_ref in sent_refs:
            size = sent_ref.shape[0]
            sent_ref[:, at] = value[start : start + size].astype(jnp.bfloat16)
            start += size

    def one_group(group, found):
        numbers = [group * GROUP + inner for inner in range(GROUP)]
        results = partial_softmax(
            numbers, query_ref, (first_key, second_key), (first_value, second_value), rows, same_row
        )
        for head, (mean, lse) in zip(numbers, results):
            store(lanes_of(head), mean)
            found = jnp.where(lane % heads == head, lse, found)
        return found

    left = lax.fori_loop(0, heads // GROUP, one_group, jnp.zeros((tokens, LANES), jnp.float32))
    packed = jnp.zeros((tokens, LANES), jnp.float32)
    for piece in range(PIECES):
        part = left.astype(jnp.bfloat16).astype(jnp.float32)
        left = left - part
        packed = jnp.where(lane // heads == piece, part, packed)
    packed = jnp.where(lane == LANES - 1, 1.0, packed)
    store(slice(width, width + LANES), packed)


def guest_attention(query, keys, values, start, sizes, after):
    tokens, width = query.shape
    return pl.pallas_call(
        functools.partial(guest_kernel, start),
        in_specs=[IN_VMEM] * 5 + [IN_PLACE],
        out_specs=[IN_VMEM] * len(sizes),
        out_shape=[jax.ShapeDtypeStruct((size, width + LANES), jnp.bfloat16) for size in sizes],
        compiler_params=pltpu.CompilerParams(vmem_limit_bytes=24 * 2**20),
        cost_estimate=pl.CostEstimate(
            flops=8 * tokens * tokens * width, bytes_accessed=12 * tokens * width, transcendentals=0
        ),
        name="guest_attention",
    )(query, *keys, *values, after)


def merge_kernel(mean_ref, lse_ref, sent_ref, *rest):
    out_ref = rest[-1]
    _, width = mean_ref.shape
    heads = width // HS
    pieces = sent_ref[:, width:].astype(jnp.float32)
    lse = pieces
    for piece in range(1, PIECES):
        lse = lse + pltpu.roll(pieces, LANES - piece * heads, 1)
    lse = jnp.where(pieces[:, LANES - 1 :] > 0, lse, NEG_FILL)
    share = 1.0 / (1.0 + jnp.exp(lse_ref[...] - lse))

    def one_group(group, share):
        for inner in range(GROUP):
            at = lanes_of(group * GROUP + inner)
            own = mean_ref[:, at]
            guest = sent_ref[:, at].astype(jnp.float32)
            out_ref[:, at] = (own + share[:, inner : inner + 1] * (guest - own)).astype(jnp.bfloat16)
        return pltpu.roll(share, LANES - GROUP, 1)

    lax.fori_loop(0, heads // GROUP, one_group, share)


def merge(mean, lse, sent, start, before):
    tokens, width = mean.shape
    part_tokens = sent.shape[0]

    def rows(lanes):
        return pl.BlockSpec((pl.Element(part_tokens), pl.Element(lanes)), lambda i: (start, 0))

    return pl.pallas_call(
        merge_kernel,
        grid=(1,),
        in_specs=[
            rows(width),
            rows(LANES),
            pl.BlockSpec((part_tokens, width + LANES), lambda i: (0, 0)),
        ]
        + [IN_PLACE] * len(before),
        out_specs=rows(width),
        out_shape=jax.ShapeDtypeStruct((tokens, width), jnp.bfloat16),
        input_output_aliases={3: 0} if before else {},
        compiler_params=pltpu.CompilerParams(vmem_limit_bytes=16 * 2**20),
        cost_estimate=pl.CostEstimate(
            flops=4 * part_tokens * width, bytes_accessed=8 * part_tokens * width, transcendentals=0
        ),
        name="merge",
    )(mean, lse, sent, *before)


def matchings(slots):
    if len(slots) < 2:
        return [[]]
    first, rest = slots[0], slots[1:]
    found = list(matchings(rest))
    for other in rest:
        left = [slot for slot in rest if slot != other]
        found += [[(first, other)] + more for more in matchings(left)]
    return found


def device_pairs(matching, slot_devices):
    ways = [way for pair in matching for way in (pair, pair[::-1])]
    return [
        (source * slot_devices + inner, target * slot_devices + inner)
        for source, target in ways
        for inner in range(slot_devices)
    ]


def prepare(request_of_slot, query, every):
    width = query.shape[1]
    part = QUERY_ROWS[0] * COLS

    def kernel(request_hbm, query_hbm, number_hbm, part_ref, request_ref, number_ref, sems):
        asked = pltpu.make_async_copy(request_hbm, request_ref, sems.at[0])
        taken = pltpu.make_async_copy(query_hbm.at[pl.ds(0, part)], part_ref, sems.at[1])
        told = pltpu.make_async_copy(number_ref, number_hbm, sems.at[2])
        asked.start()
        taken.start()
        asked.wait()
        chosen = jnp.int32(0)
        for number, matching in enumerate(every):
            fits = functools.reduce(
                jnp.logical_and, [request_ref[one] == request_ref[other] for one, other in matching]
            )
            chosen = jnp.where(fits, jnp.int32(number), chosen)
        number_ref[0] = chosen
        told.start()
        taken.wait()
        told.wait()

    number, first_part = pl.pallas_call(
        kernel,
        in_specs=[IN_PLACE] * 2,
        out_specs=[IN_PLACE, IN_VMEM],
        out_shape=[
            jax.ShapeDtypeStruct((1,), jnp.int32),
            jax.ShapeDtypeStruct((part, width), query.dtype),
        ],
        scratch_shapes=[
            pltpu.SMEM(request_of_slot.shape, jnp.int32),
            pltpu.SMEM((1,), jnp.int32),
            pltpu.SemaphoreType.DMA((3,)),
        ],
        name="prepare",
    )(request_of_slot, query)
    return number[0], first_part


def few_slots(query_vectors, key_vectors, value_vectors, request_of_slot):
    device_count = lax.axis_size("view")
    slot_count = request_of_slot.shape[0]
    slot_devices = device_count // slot_count
    token_count = ROWS * COLS
    width = HEADS * HS
    query = query_vectors.reshape(token_count, width)
    key = key_vectors.reshape(token_count, width)
    value = value_vectors.reshape(token_count, width)
    every = [matching for matching in matchings(list(range(slot_count))) if matching]
    branch, first_part = prepare(request_of_slot, query, every)

    def exchange(matching):
        pairs = device_pairs(matching, slot_devices)

        def run(key, value, query, first_part):
            return pair_attention(key, value, query, first_part)

        def pair_attention(key, value, query, first_part):
            guests = [lax.ppermute(first_part, "view", pairs)]
            start = first_part.shape[0]
            for rows in QUERY_ROWS[1:]:
                sent = lax.slice_in_dim(query, start, start + rows * COLS)
                guests.append(lax.ppermute(sent, "view", pairs))
                start += rows * COLS
            keys = (key, partner(key, "view", 0))
            values = (value, partner(value, "view", 0))
            mean, lse = own_attention(query, keys, values)
            backs, start = [], 0
            for guest, rows in zip(guests, RETURN_ROWS):
                sizes = [row * COLS for row in rows]
                for sent in guest_attention(guest, keys, values, start, sizes, lse):
                    backs.append(lax.ppermute(sent, "view", pairs))
                start += guest.shape[0]
            out, start = (), 0
            for back in backs:
                out = (merge(mean, lse, back, start, out),)
                start += back.shape[0]
            return out[0]

        return run

    branches = [exchange(matching) for matching in every]
    attended = lax.switch(branch, branches, key, value, query, first_part)
    return attended.reshape(1, ROWS, COLS, HEADS * HS)


def shards(query_vectors, key_vectors, value_vectors, request_of_slot):
    most_views = request_of_slot.shape[0] // 2
    path = few_slots if most_views == 2 else many_slots
    return path(query_vectors, key_vectors, value_vectors, request_of_slot)


def solution(mesh):
    return jax.shard_map(
        shards,
        mesh=mesh,
        in_specs=(
            P(("groups", "view"), None, None, None),
            P(("groups", "view"), None, None, None),
            P(("groups", "view"), None, None, None),
            P("groups"),
        ),
        out_specs=P(("groups", "view"), None, None, None),
        check_vma=False,
    )
```

```python
import functools

import jax
import jax.numpy as jnp
from jax import lax
from jax.experimental import pallas as pl
from jax.experimental.pallas import tpu as pltpu
from jax.sharding import PartitionSpec as P


HEADS = 32
HS = 128
ROWS = 16
COLS = 8


NEG_FILL = -1e30


def partner(value, axis, distance):
    return lax.ppermute(value, axis, [(i, i ^ 1 << distance) for i in range(lax.axis_size(axis))])


def masked_softmax(scores, allowed):
    scores = jnp.where(allowed, scores, NEG_FILL)
    maximum = jnp.max(scores, axis=-1)
    raised = jnp.exp(scores - maximum[..., None])
    totals = jnp.sum(raised, axis=-1)
    return (maximum, totals, raised.astype(jnp.bfloat16))


def combine(first_part, second_part):
    highest = jnp.maximum(first_part[0], second_part[0])
    first_scale = jnp.exp(first_part[0] - highest)
    second_scale = jnp.exp(second_part[0] - highest)
    denominator = first_part[1] * first_scale + second_part[1] * second_scale
    numerator = first_part[2] * first_scale[..., None] + second_part[2] * second_scale[..., None]
    return (numerator / denominator[..., None]).astype(jnp.bfloat16)


def into_rows(tensor, row_blocks, head_groups):
    trailing = tensor.shape[3:]
    block_rows = tensor.shape[0] // row_blocks
    width_cols = tensor.shape[1]
    group_heads = tensor.shape[2] // head_groups
    shaped = tensor.reshape(
        (row_blocks, block_rows, width_cols, head_groups, group_heads) + trailing
    )
    permuted = (0, 3, 1, 2, 4) + tuple(range(5, 5 + len(trailing)))
    return shaped.transpose(permuted).reshape(
        (row_blocks * head_groups, block_rows, width_cols, group_heads) + trailing
    )


def into_tokens(tensor, row_blocks, head_groups):
    trailing = tensor.shape[4:]
    block_rows = tensor.shape[1]
    width_cols = tensor.shape[2]
    group_heads = tensor.shape[3]
    shaped = tensor.reshape(
        (row_blocks, head_groups, block_rows, width_cols, group_heads) + trailing
    )
    permuted = (0, 2, 3, 1, 4) + tuple(range(5, 5 + len(trailing)))
    return shaped.transpose(permuted).reshape(
        (row_blocks * block_rows * width_cols, head_groups * group_heads) + trailing
    )


def many_slots(query_vectors, key_vectors, value_vectors, request_of_slot):
    scaling = HS ** (-0.5)
    token_count = ROWS * COLS
    partner_key, partner_value = partner((key_vectors, value_vectors), "view", 0)
    head_blocks = 4
    block_heads = HEADS // head_blocks
    own_query = query_vectors.reshape(token_count, head_blocks, block_heads, HS)
    both_keys = jnp.concatenate(
        [
            key_vectors.reshape(token_count, head_blocks, block_heads, HS),
            partner_key.reshape(token_count, head_blocks, block_heads, HS),
        ],
        axis=0,
    )
    both_values = jnp.concatenate(
        [
            value_vectors.reshape(token_count, head_blocks, block_heads, HS),
            partner_value.reshape(token_count, head_blocks, block_heads, HS),
        ],
        axis=0,
    )
    query_row = jnp.arange(token_count) // COLS
    key_row = jnp.arange(2 * token_count) % token_count // COLS
    local_allowed = query_row[:, None] != key_row[None, :]

    def local_block(triple):
        block_scores = (
            jnp.einsum("nhx,khx->hnk", triple[0], triple[1], preferred_element_type=jnp.float32)
            * scaling
        )
        block_peak, block_total, block_weights = masked_softmax(block_scores, local_allowed[None])
        block_sum = jnp.einsum(
            "hnk,khx->nhx", block_weights, triple[2], preferred_element_type=jnp.float32
        )
        return (block_peak.T, block_total.T, block_sum)

    block_peaks, block_totals, block_sums = lax.map(
        local_block,
        (
            jnp.moveaxis(own_query, 1, 0),
            jnp.moveaxis(both_keys, 1, 0),
            jnp.moveaxis(both_values, 1, 0),
        ),
    )
    local_peak = jnp.moveaxis(block_peaks, 0, 1).reshape(token_count, HEADS)
    local_total = jnp.moveaxis(block_totals, 0, 1).reshape(token_count, HEADS)
    local_sum = jnp.moveaxis(block_sums, 0, 1).reshape(token_count, HEADS, HS)
    device_count = lax.axis_size("view")
    slot_count = device_count // 4
    pass_images = device_count // 2
    head_groups = 8
    row_blocks = device_count // head_groups
    block_rows = ROWS // row_blocks
    slot_request = jnp.broadcast_to(
        request_of_slot[:, None], (request_of_slot.shape[0], 2 * COLS)
    ).reshape(-1)
    row_allowed = slot_request[:, None] == slot_request[None, :]

    def arrange(tensor):
        shaped = tensor.reshape(slot_count, 2, 2, block_rows, COLS, HS).transpose(1, 3, 0, 2, 4, 5)
        return shaped.reshape(2 * block_rows, pass_images * COLS, HS)

    def restore(tensor):
        trailing = tensor.shape[2:]
        shaped = tensor.reshape((2, block_rows, slot_count, 2, COLS) + trailing)
        permuted = (2, 0, 3, 1, 4) + tuple(range(5, 5 + len(trailing)))
        return shaped.transpose(permuted).reshape((device_count, block_rows, COLS) + trailing)

    def one_head(triple):
        row_scores = (
            jnp.einsum(
                "bnx,bkx->bnk",
                arrange(triple[0]),
                arrange(triple[1]),
                preferred_element_type=jnp.float32,
            )
            * scaling
        )
        row_peak, row_total, row_weights = masked_softmax(row_scores, row_allowed[None])
        row_sum = jnp.einsum(
            "bnk,bkx->bnx", row_weights, arrange(triple[2]), preferred_element_type=jnp.float32
        )
        return (restore(row_peak), restore(row_total), restore(row_sum))

    query_rows = into_rows(query_vectors.reshape(ROWS, COLS, HEADS, HS), row_blocks, head_groups)
    key_rows = into_rows(key_vectors.reshape(ROWS, COLS, HEADS, HS), row_blocks, head_groups)
    value_rows = into_rows(value_vectors.reshape(ROWS, COLS, HEADS, HS), row_blocks, head_groups)
    by_head = (
        jnp.moveaxis(
            lax.all_to_all(query_rows, "view", split_axis=0, concat_axis=0, tiled=True), 3, 0
        ),
        jnp.moveaxis(
            lax.all_to_all(key_rows, "view", split_axis=0, concat_axis=0, tiled=True), 3, 0
        ),
        jnp.moveaxis(
            lax.all_to_all(value_rows, "view", split_axis=0, concat_axis=0, tiled=True), 3, 0
        ),
    )
    row_peaks, row_totals, row_sums = lax.map(one_head, by_head)
    peak_part = jnp.moveaxis(row_peaks, 0, 3)
    total_part = jnp.moveaxis(row_totals, 0, 3)
    sum_part = jnp.moveaxis(row_sums, 0, 3)
    row_peak = lax.all_to_all(peak_part, "view", split_axis=0, concat_axis=0, tiled=True)
    row_total = lax.all_to_all(total_part, "view", split_axis=0, concat_axis=0, tiled=True)
    row_sum = lax.all_to_all(sum_part, "view", split_axis=0, concat_axis=0, tiled=True)
    row_peak = into_tokens(row_peak, row_blocks, head_groups)
    row_total = into_tokens(row_total, row_blocks, head_groups)
    row_sum = into_tokens(row_sum, row_blocks, head_groups)
    attended = combine((local_peak, local_total, local_sum), (row_peak, row_total, row_sum))
    return attended.reshape(1, ROWS, COLS, HEADS * HS)


SCALING = HS ** (-0.5)
LANES = 128
MARKER = 8
GROUP = 8
QUERY_ROWS = (8, 8)
RETURN_ROWS = ((8,), (6, 2))
IN_VMEM = pl.BlockSpec(memory_space=pltpu.VMEM)
IN_PLACE = pl.BlockSpec(memory_space=pl.ANY)


def scores_of(query, keys):
    return lax.dot_general(query, keys, (((1,), (1,)), ((), ())), preferred_element_type=jnp.float32)


def lanes_of(head):
    return pl.ds(pl.multiple_of(head * HS, HS), HS)


def partial_softmax(heads, query_ref, key_refs, value_refs, rows, allowed):
    scores = []
    for head in heads:
        at = lanes_of(head)
        keys = jnp.concatenate([ref[rows, at] for ref in key_refs], axis=0)
        scores.append(scores_of(query_ref[:, at], keys))
    if allowed is not None:
        scores = [jnp.where(allowed, score, NEG_FILL) for score in scores]
    peaks = [jnp.max(score, axis=1, keepdims=True) for score in scores]
    weights = [
        jnp.exp((score - peak) * SCALING).astype(jnp.bfloat16)
        for score, peak in zip(scores, peaks)
    ]
    results = []
    for head, peak, weight in zip(heads, peaks, weights):
        at = lanes_of(head)
        values = jnp.concatenate([ref[rows, at] for ref in value_refs], axis=0)
        ones = jnp.ones_like(values)
        both = jnp.dot(
            weight, jnp.concatenate([values, ones], axis=1), preferred_element_type=jnp.float32
        )
        total = both[:, HS:]
        results.append((both[:, :HS] / total, peak * SCALING + jnp.log(total)))
    return results


def own_kernel(query_ref, first_key, second_key, first_value, second_value, mean_ref, lse_ref):
    heads = query_ref.shape[1] // HS
    lane = lax.broadcasted_iota(jnp.int32, lse_ref.shape, 1)

    def one_group(group, found):
        numbers = [group * GROUP + inner for inner in range(GROUP)]
        results = partial_softmax(
            numbers, query_ref, (first_key, second_key), (first_value, second_value), slice(None), None
        )
        for head, (mean, lse) in zip(numbers, results):
            mean_ref[:, lanes_of(head)] = mean
            found = jnp.where(lane == head, lse, found)
        return found

    zeros = jnp.zeros(lse_ref.shape, jnp.float32)
    lse_ref[...] = lax.fori_loop(0, heads // GROUP, one_group, zeros)


def own_attention(query, keys, values):
    tokens, width = query.shape
    return pl.pallas_call(
        own_kernel,
        out_shape=[
            jax.ShapeDtypeStruct((tokens, width), jnp.float32),
            jax.ShapeDtypeStruct((tokens, LANES), jnp.float32),
        ],
        compiler_params=pltpu.CompilerParams(vmem_limit_bytes=24 * 2**20),
        cost_estimate=pl.CostEstimate(
            flops=8 * tokens * tokens * width, bytes_accessed=14 * tokens * width, transcendentals=0
        ),
        name="own_attention",
    )(query, *keys, *values)


def rows_of(head, tokens):
    return pl.ds(pl.multiple_of(head * tokens, tokens), tokens)


def guest_kernel(start, query_ref, first_key, second_key, first_value, second_value, _, *sent_refs):
    tokens, width = query_ref.shape
    heads = width // HS
    rows = slice(start, start + tokens)
    shape = (tokens, 2 * tokens)
    query_row = lax.broadcasted_iota(jnp.int32, shape, 0) // COLS
    key_row = lax.broadcasted_iota(jnp.int32, shape, 1) % tokens // COLS
    same_row = query_row == key_row
    lane = lax.broadcasted_iota(jnp.int32, (tokens, LANES), 1)
    firsts = [0]
    for sent_ref in sent_refs[1:]:
        firsts.append(tokens - sent_ref.shape[0] // heads)
    sizes = [stop - first for first, stop in zip(firsts, firsts[1:] + [tokens])]

    def one_group(group, found):
        numbers = [group * GROUP + inner for inner in range(GROUP)]
        results = partial_softmax(
            numbers, query_ref, (first_key, second_key), (first_value, second_value), rows, same_row
        )
        for head, (mean, lse) in zip(numbers, results):
            for sent_ref, first, size in zip(sent_refs, firsts, sizes):
                part = mean[first : first + size].astype(jnp.bfloat16)
                sent_ref[rows_of(head, size), :] = part
            found = jnp.where(lane % heads == head, lse, found)
        return found

    found = lax.fori_loop(0, heads // GROUP, one_group, jnp.zeros((tokens, LANES), jnp.float32))
    high = found.astype(jnp.bfloat16).astype(jnp.float32)
    pieces = jnp.where(lane // heads % 2 == 0, high, found - high)
    half, at = tokens // 2, heads * sizes[0]
    packed = jnp.where(lane[:half] < LANES // 2, pieces[:half], pieces[half:])
    sent_refs[0][at : at + half, :] = packed.astype(jnp.bfloat16)
    sent_refs[0][at + half :, :] = jnp.ones((MARKER, LANES), jnp.bfloat16)


def guest_attention(query, keys, values, start, sizes, after):
    tokens, width = query.shape
    heads = width // HS
    lengths = [heads * size for size in sizes]
    lengths[0] += tokens // 2 + MARKER
    return pl.pallas_call(
        functools.partial(guest_kernel, start),
        in_specs=[IN_VMEM] * 5 + [IN_PLACE],
        out_specs=[IN_VMEM] * len(sizes),
        out_shape=[jax.ShapeDtypeStruct((length, LANES), jnp.bfloat16) for length in lengths],
        compiler_params=pltpu.CompilerParams(vmem_limit_bytes=24 * 2**20),
        cost_estimate=pl.CostEstimate(
            flops=8 * tokens * tokens * width, bytes_accessed=12 * tokens * width, transcendentals=0
        ),
        name="guest_attention",
    )(query, *keys, *values, after)


def merge_kernel(mean_ref, lse_ref, sent_ref, *rest):
    out_ref, left_refs = (rest[-3], rest[-2:]) if len(rest) > 2 else (rest[-1], ())
    tokens, width = mean_ref.shape
    size = out_ref.shape[0]
    heads = width // HS
    half, at = tokens // 2, heads * size
    pieces = sent_ref[at : at + half, :].astype(jnp.float32)
    lse = pieces + pltpu.roll(pieces, LANES - heads, 1)
    lse = jnp.concatenate([lse, pltpu.roll(lse, LANES // 2, 1)], axis=0)
    received = sent_ref[at + half : at + half + 1, :].astype(jnp.float32) > 0
    share = 1.0 / (1.0 + jnp.exp(lse_ref[...] - jnp.where(received, lse, NEG_FILL)))

    def one_group(group, share):
        for inner in range(GROUP):
            head = group * GROUP + inner
            lanes = lanes_of(head)
            part = share[:, inner : inner + 1]
            own = mean_ref[:size, lanes]
            guest = sent_ref[rows_of(head, size), :].astype(jnp.float32)
            out_ref[:, lanes] = (own + part[:size] * (guest - own)).astype(jnp.bfloat16)
            if left_refs:
                later = jnp.broadcast_to(part[size:], (tokens - size, HS))
                own = mean_ref[size:, lanes]
                left_refs[0][:, lanes] = own - later * own
                left_refs[1][:, lanes] = later
        return pltpu.roll(share, LANES - GROUP, 1)

    lax.fori_loop(0, heads // GROUP, one_group, share)


def last_kernel(scaled_ref, share_ref, sent_ref, _, out_ref):
    size, width = scaled_ref.shape
    for head in range(width // HS):
        lanes = slice(head * HS, (head + 1) * HS)
        guest = sent_ref[head * size : (head + 1) * size, :].astype(jnp.float32)
        out_ref[:, lanes] = (scaled_ref[:, lanes] + share_ref[:, lanes] * guest).astype(jnp.bfloat16)


def token_rows(first, size, width):
    return pl.BlockSpec((pl.Element(size), pl.Element(width)), lambda i: (first, 0))


def whole(shape):
    return pl.BlockSpec(shape, lambda i: (0, 0))


def merge(mean, lse, backs, start, sizes, before):
    total, width = mean.shape
    tokens = sum(sizes)
    size, later = sizes[0], sizes[1:]
    left = [jax.ShapeDtypeStruct((later[0], width), jnp.float32)] * 2 if later else []
    result = jax.ShapeDtypeStruct((total, width), jnp.bfloat16)
    params = pltpu.CompilerParams(vmem_limit_bytes=16 * 2**20)
    out, *left = pl.pallas_call(
        merge_kernel,
        grid=(1,),
        in_specs=[
            token_rows(start, tokens, width),
            token_rows(start, tokens, LANES),
            whole(backs[0].shape),
        ]
        + [IN_PLACE] * len(before),
        out_specs=[token_rows(start, size, width)] + [whole(part.shape) for part in left],
        out_shape=[result] + left,
        input_output_aliases={3: 0} if before else {},
        compiler_params=params,
        cost_estimate=pl.CostEstimate(
            flops=4 * tokens * width, bytes_accessed=8 * tokens * width, transcendentals=0
        ),
        name="merge",
    )(mean, lse, backs[0], *before)
    if not later:
        return out
    return pl.pallas_call(
        last_kernel,
        grid=(1,),
        in_specs=[whole(left[0].shape), whole(left[1].shape), whole(backs[1].shape), IN_PLACE],
        out_specs=token_rows(start + size, later[0], width),
        out_shape=result,
        input_output_aliases={3: 0},
        compiler_params=params,
        name="last_merge",
    )(*left, backs[1], out)


def matchings(slots):
    if len(slots) < 2:
        return [[]]
    first, rest = slots[0], slots[1:]
    found = list(matchings(rest))
    for other in rest:
        left = [slot for slot in rest if slot != other]
        found += [[(first, other)] + more for more in matchings(left)]
    return found


def device_pairs(matching, slot_devices):
    ways = [way for pair in matching for way in (pair, pair[::-1])]
    return [
        (source * slot_devices + inner, target * slot_devices + inner)
        for source, target in ways
        for inner in range(slot_devices)
    ]


def prepare(request_of_slot, query, every):
    width = query.shape[1]
    part = QUERY_ROWS[0] * COLS

    def kernel(request_hbm, query_hbm, number_hbm, part_ref, request_ref, number_ref, sems):
        asked = pltpu.make_async_copy(request_hbm, request_ref, sems.at[0])
        taken = pltpu.make_async_copy(query_hbm.at[pl.ds(0, part)], part_ref, sems.at[1])
        told = pltpu.make_async_copy(number_ref, number_hbm, sems.at[2])
        asked.start()
        taken.start()
        asked.wait()
        chosen = jnp.int32(0)
        for number, matching in enumerate(every):
            fits = functools.reduce(
                jnp.logical_and, [request_ref[one] == request_ref[other] for one, other in matching]
            )
            chosen = jnp.where(fits, jnp.int32(number), chosen)
        number_ref[0] = chosen
        told.start()
        taken.wait()
        told.wait()

    number, first_part = pl.pallas_call(
        kernel,
        in_specs=[IN_PLACE] * 2,
        out_specs=[IN_PLACE, IN_VMEM],
        out_shape=[
            jax.ShapeDtypeStruct((1,), jnp.int32),
            jax.ShapeDtypeStruct((part, width), query.dtype),
        ],
        scratch_shapes=[
            pltpu.SMEM(request_of_slot.shape, jnp.int32),
            pltpu.SMEM((1,), jnp.int32),
            pltpu.SemaphoreType.DMA((3,)),
        ],
        name="prepare",
    )(request_of_slot, query)
    return number[0], first_part


def few_slots(query_vectors, key_vectors, value_vectors, request_of_slot):
    device_count = lax.axis_size("view")
    slot_count = request_of_slot.shape[0]
    slot_devices = device_count // slot_count
    token_count = ROWS * COLS
    width = HEADS * HS
    query = query_vectors.reshape(token_count, width)
    key = key_vectors.reshape(token_count, width)
    value = value_vectors.reshape(token_count, width)
    every = [matching for matching in matchings(list(range(slot_count))) if matching]
    branch, first_part = prepare(request_of_slot, query, every)

    def exchange(matching):
        pairs = device_pairs(matching, slot_devices)

        def run(key, value, query, first_part):
            return pair_attention(key, value, query, first_part)

        def pair_attention(key, value, query, first_part):
            guests = [lax.ppermute(first_part, "view", pairs)]
            start = first_part.shape[0]
            for rows in QUERY_ROWS[1:]:
                sent = lax.slice_in_dim(query, start, start + rows * COLS)
                guests.append(lax.ppermute(sent, "view", pairs))
                start += rows * COLS
            keys = (key, partner(key, "view", 0))
            values = (value, partner(value, "view", 0))
            mean, lse = own_attention(query, keys, values)
            returns, start = [], 0
            for guest, rows in zip(guests, RETURN_ROWS):
                sizes = [row * COLS for row in rows]
                sent = guest_attention(guest, keys, values, start, sizes, lse)
                backs = [lax.ppermute(part, "view", pairs) for part in sent]
                returns.append((backs, start, sizes))
                start += guest.shape[0]
            out = ()
            for backs, start, sizes in returns:
                out = (merge(mean, lse, backs, start, sizes, out),)
            return out[0]

        return run

    branches = [exchange(matching) for matching in every]
    attended = lax.switch(branch, branches, key, value, query, first_part)
    return attended.reshape(1, ROWS, COLS, HEADS * HS)


def shards(query_vectors, key_vectors, value_vectors, request_of_slot):
    most_views = request_of_slot.shape[0] // 2
    path = few_slots if most_views == 2 else many_slots
    return path(query_vectors, key_vectors, value_vectors, request_of_slot)


def solution(mesh):
    return jax.shard_map(
        shards,
        mesh=mesh,
        in_specs=(
            P(("groups", "view"), None, None, None),
            P(("groups", "view"), None, None, None),
            P(("groups", "view"), None, None, None),
            P("groups"),
        ),
        out_specs=P(("groups", "view"), None, None, None),
        check_vma=False,
    )
```

```python
import functools

import jax
import jax.numpy as jnp
from jax import lax
from jax.experimental import pallas as pl
from jax.experimental.pallas import tpu as pltpu
from jax.sharding import PartitionSpec as P


HEADS = 32
HS = 128
ROWS = 16
COLS = 8


NEG_FILL = -1e30


def partner(value, axis, distance):
    return lax.ppermute(value, axis, [(i, i ^ 1 << distance) for i in range(lax.axis_size(axis))])


def masked_softmax(scores, allowed):
    scores = jnp.where(allowed, scores, NEG_FILL)
    maximum = jnp.max(scores, axis=-1)
    raised = jnp.exp(scores - maximum[..., None])
    totals = jnp.sum(raised, axis=-1)
    return (maximum, totals, raised.astype(jnp.bfloat16))


def combine(first_part, second_part):
    highest = jnp.maximum(first_part[0], second_part[0])
    first_scale = jnp.exp(first_part[0] - highest)
    second_scale = jnp.exp(second_part[0] - highest)
    denominator = first_part[1] * first_scale + second_part[1] * second_scale
    numerator = first_part[2] * first_scale[..., None] + second_part[2] * second_scale[..., None]
    return (numerator / denominator[..., None]).astype(jnp.bfloat16)


def into_rows(tensor, row_blocks, head_groups):
    trailing = tensor.shape[3:]
    block_rows = tensor.shape[0] // row_blocks
    width_cols = tensor.shape[1]
    group_heads = tensor.shape[2] // head_groups
    shaped = tensor.reshape(
        (row_blocks, block_rows, width_cols, head_groups, group_heads) + trailing
    )
    permuted = (0, 3, 1, 2, 4) + tuple(range(5, 5 + len(trailing)))
    return shaped.transpose(permuted).reshape(
        (row_blocks * head_groups, block_rows, width_cols, group_heads) + trailing
    )


def into_tokens(tensor, row_blocks, head_groups):
    trailing = tensor.shape[4:]
    block_rows = tensor.shape[1]
    width_cols = tensor.shape[2]
    group_heads = tensor.shape[3]
    shaped = tensor.reshape(
        (row_blocks, head_groups, block_rows, width_cols, group_heads) + trailing
    )
    permuted = (0, 2, 3, 1, 4) + tuple(range(5, 5 + len(trailing)))
    return shaped.transpose(permuted).reshape(
        (row_blocks * block_rows * width_cols, head_groups * group_heads) + trailing
    )


def many_slots(query_vectors, key_vectors, value_vectors, request_of_slot):
    scaling = HS ** (-0.5)
    token_count = ROWS * COLS
    partner_key, partner_value = partner((key_vectors, value_vectors), "view", 0)
    head_blocks = 4
    block_heads = HEADS // head_blocks
    own_query = query_vectors.reshape(token_count, head_blocks, block_heads, HS)
    both_keys = jnp.concatenate(
        [
            key_vectors.reshape(token_count, head_blocks, block_heads, HS),
            partner_key.reshape(token_count, head_blocks, block_heads, HS),
        ],
        axis=0,
    )
    both_values = jnp.concatenate(
        [
            value_vectors.reshape(token_count, head_blocks, block_heads, HS),
            partner_value.reshape(token_count, head_blocks, block_heads, HS),
        ],
        axis=0,
    )
    query_row = jnp.arange(token_count) // COLS
    key_row = jnp.arange(2 * token_count) % token_count // COLS
    local_allowed = query_row[:, None] != key_row[None, :]

    def local_block(triple):
        block_scores = (
            jnp.einsum("nhx,khx->hnk", triple[0], triple[1], preferred_element_type=jnp.float32)
            * scaling
        )
        block_peak, block_total, block_weights = masked_softmax(block_scores, local_allowed[None])
        block_sum = jnp.einsum(
            "hnk,khx->nhx", block_weights, triple[2], preferred_element_type=jnp.float32
        )
        return (block_peak.T, block_total.T, block_sum)

    block_peaks, block_totals, block_sums = lax.map(
        local_block,
        (
            jnp.moveaxis(own_query, 1, 0),
            jnp.moveaxis(both_keys, 1, 0),
            jnp.moveaxis(both_values, 1, 0),
        ),
    )
    local_peak = jnp.moveaxis(block_peaks, 0, 1).reshape(token_count, HEADS)
    local_total = jnp.moveaxis(block_totals, 0, 1).reshape(token_count, HEADS)
    local_sum = jnp.moveaxis(block_sums, 0, 1).reshape(token_count, HEADS, HS)
    device_count = lax.axis_size("view")
    slot_count = device_count // 4
    pass_images = device_count // 2
    head_groups = 8
    row_blocks = device_count // head_groups
    block_rows = ROWS // row_blocks
    slot_request = jnp.broadcast_to(
        request_of_slot[:, None], (request_of_slot.shape[0], 2 * COLS)
    ).reshape(-1)
    row_allowed = slot_request[:, None] == slot_request[None, :]

    def arrange(tensor):
        shaped = tensor.reshape(slot_count, 2, 2, block_rows, COLS, HS).transpose(1, 3, 0, 2, 4, 5)
        return shaped.reshape(2 * block_rows, pass_images * COLS, HS)

    def restore(tensor):
        trailing = tensor.shape[2:]
        shaped = tensor.reshape((2, block_rows, slot_count, 2, COLS) + trailing)
        permuted = (2, 0, 3, 1, 4) + tuple(range(5, 5 + len(trailing)))
        return shaped.transpose(permuted).reshape((device_count, block_rows, COLS) + trailing)

    def one_head(triple):
        row_scores = (
            jnp.einsum(
                "bnx,bkx->bnk",
                arrange(triple[0]),
                arrange(triple[1]),
                preferred_element_type=jnp.float32,
            )
            * scaling
        )
        row_peak, row_total, row_weights = masked_softmax(row_scores, row_allowed[None])
        row_sum = jnp.einsum(
            "bnk,bkx->bnx", row_weights, arrange(triple[2]), preferred_element_type=jnp.float32
        )
        return (restore(row_peak), restore(row_total), restore(row_sum))

    query_rows = into_rows(query_vectors.reshape(ROWS, COLS, HEADS, HS), row_blocks, head_groups)
    key_rows = into_rows(key_vectors.reshape(ROWS, COLS, HEADS, HS), row_blocks, head_groups)
    value_rows = into_rows(value_vectors.reshape(ROWS, COLS, HEADS, HS), row_blocks, head_groups)
    by_head = (
        jnp.moveaxis(
            lax.all_to_all(query_rows, "view", split_axis=0, concat_axis=0, tiled=True), 3, 0
        ),
        jnp.moveaxis(
            lax.all_to_all(key_rows, "view", split_axis=0, concat_axis=0, tiled=True), 3, 0
        ),
        jnp.moveaxis(
            lax.all_to_all(value_rows, "view", split_axis=0, concat_axis=0, tiled=True), 3, 0
        ),
    )
    row_peaks, row_totals, row_sums = lax.map(one_head, by_head)
    peak_part = jnp.moveaxis(row_peaks, 0, 3)
    total_part = jnp.moveaxis(row_totals, 0, 3)
    sum_part = jnp.moveaxis(row_sums, 0, 3)
    row_peak = lax.all_to_all(peak_part, "view", split_axis=0, concat_axis=0, tiled=True)
    row_total = lax.all_to_all(total_part, "view", split_axis=0, concat_axis=0, tiled=True)
    row_sum = lax.all_to_all(sum_part, "view", split_axis=0, concat_axis=0, tiled=True)
    row_peak = into_tokens(row_peak, row_blocks, head_groups)
    row_total = into_tokens(row_total, row_blocks, head_groups)
    row_sum = into_tokens(row_sum, row_blocks, head_groups)
    attended = combine((local_peak, local_total, local_sum), (row_peak, row_total, row_sum))
    return attended.reshape(1, ROWS, COLS, HEADS * HS)


SCALING = HS ** (-0.5)
LANES = 128
MARKER = 8
PIECES = 2
GROUP = 8
QUERY_ROWS = (8, 8)
RETURN_ROWS = ((8,), (6, 2))
IN_VMEM = pl.BlockSpec(memory_space=pltpu.VMEM)
IN_PLACE = pl.BlockSpec(memory_space=pl.ANY)


def scores_of(query, keys):
    return lax.dot_general(query, keys, (((1,), (1,)), ((), ())), preferred_element_type=jnp.float32)


def lanes_of(head):
    return pl.ds(pl.multiple_of(head * HS, HS), HS)


def partial_softmax(heads, query_ref, key_refs, value_refs, rows, allowed):
    scores = []
    for head in heads:
        at = lanes_of(head)
        keys = jnp.concatenate([ref[rows, at] for ref in key_refs], axis=0)
        scores.append(scores_of(query_ref[:, at], keys))
    if allowed is not None:
        scores = [jnp.where(allowed, score, NEG_FILL) for score in scores]
    peaks = [jnp.max(score, axis=1, keepdims=True) for score in scores]
    weights = [
        jnp.exp((score - peak) * SCALING).astype(jnp.bfloat16)
        for score, peak in zip(scores, peaks)
    ]
    results = []
    for head, peak, weight in zip(heads, peaks, weights):
        at = lanes_of(head)
        values = jnp.concatenate([ref[rows, at] for ref in value_refs], axis=0)
        ones = jnp.ones_like(values)
        both = jnp.dot(
            weight, jnp.concatenate([values, ones], axis=1), preferred_element_type=jnp.float32
        )
        total = both[:, HS:]
        results.append((both[:, :HS] / total, peak * SCALING + jnp.log(total)))
    return results


def own_kernel(query_ref, first_key, second_key, first_value, second_value, mean_ref, lse_ref):
    heads = query_ref.shape[1] // HS
    lane = lax.broadcasted_iota(jnp.int32, lse_ref.shape, 1)

    def one_group(group, found):
        numbers = [group * GROUP + inner for inner in range(GROUP)]
        results = partial_softmax(
            numbers, query_ref, (first_key, second_key), (first_value, second_value), slice(None), None
        )
        for head, (mean, lse) in zip(numbers, results):
            mean_ref[:, lanes_of(head)] = mean
            found = jnp.where(lane == head, lse, found)
        return found

    zeros = jnp.zeros(lse_ref.shape, jnp.float32)
    lse_ref[...] = lax.fori_loop(0, heads // GROUP, one_group, zeros)


def own_attention(query, keys, values):
    tokens, width = query.shape
    return pl.pallas_call(
        own_kernel,
        out_shape=[
            jax.ShapeDtypeStruct((tokens, width), jnp.float32),
            jax.ShapeDtypeStruct((tokens, LANES), jnp.float32),
        ],
        compiler_params=pltpu.CompilerParams(vmem_limit_bytes=24 * 2**20),
        cost_estimate=pl.CostEstimate(
            flops=8 * tokens * tokens * width, bytes_accessed=14 * tokens * width, transcendentals=0
        ),
        name="own_attention",
    )(query, *keys, *values)


def rows_of(head, tokens):
    return pl.ds(pl.multiple_of(head * tokens, tokens), tokens)


def guest_kernel(start, matched, query_ref, first_key, second_key, first_value, second_value, _, *sent_refs):
    tokens, width = query_ref.shape
    heads = width // HS
    rows = slice(start, start + tokens)
    shape = (tokens, 2 * tokens)
    query_row = lax.broadcasted_iota(jnp.int32, shape, 0) // COLS
    key_row = lax.broadcasted_iota(jnp.int32, shape, 1) % tokens // COLS
    same_row = query_row == key_row
    lane = lax.broadcasted_iota(jnp.int32, (tokens, LANES), 1)
    firsts = [0]
    for sent_ref in sent_refs[1:]:
        firsts.append(tokens - sent_ref.shape[0] // heads)
    sizes = [stop - first for first, stop in zip(firsts, firsts[1:] + [tokens])]

    def one_group(group, found):
        numbers = [group * GROUP + inner for inner in range(GROUP)]
        results = partial_softmax(
            numbers, query_ref, (first_key, second_key), (first_value, second_value), rows, same_row
        )
        for head, (mean, lse) in zip(numbers, results):
            for sent_ref, first, size in zip(sent_refs, firsts, sizes):
                part = mean[first : first + size].astype(jnp.bfloat16)
                sent_ref[rows_of(head, size), :] = part
            found = jnp.where(lane % heads == head, lse, found)
        return found

    found = lax.fori_loop(0, heads // GROUP, one_group, jnp.zeros((tokens, LANES), jnp.float32))
    high = found.astype(jnp.bfloat16).astype(jnp.float32)
    pieces = jnp.where(lane // heads % 2 == 0, high, found - high)
    half, at = tokens // 2, heads * sizes[0]
    packed = jnp.where(lane[:half] < LANES // 2, pieces[:half], pieces[half:])
    sent_refs[0][at : at + half, :] = packed.astype(jnp.bfloat16)
    marker = jnp.full((MARKER, LANES), matched[0], jnp.int32)
    sent_refs[0][at + half :, :] = marker.astype(jnp.float32).astype(jnp.bfloat16)


def guest_attention(matched, query, keys, values, start, sizes, after):
    tokens, width = query.shape
    heads = width // HS
    lengths = [heads * size for size in sizes]
    lengths[0] += tokens // 2 + MARKER
    return pl.pallas_call(
        functools.partial(guest_kernel, start),
        in_specs=[pl.BlockSpec(memory_space=pltpu.SMEM)] + [IN_VMEM] * 5 + [IN_PLACE],
        out_specs=[IN_VMEM] * len(sizes),
        out_shape=[jax.ShapeDtypeStruct((length, LANES), jnp.bfloat16) for length in lengths],
        compiler_params=pltpu.CompilerParams(vmem_limit_bytes=24 * 2**20),
        cost_estimate=pl.CostEstimate(
            flops=8 * tokens * tokens * width, bytes_accessed=12 * tokens * width, transcendentals=0
        ),
        name="guest_attention",
    )(matched, query, *keys, *values, after)


def merge_kernel(mean_ref, lse_ref, sent_ref, *rest):
    out_ref, left_refs = (rest[-3], rest[-2:]) if len(rest) > 2 else (rest[-1], ())
    tokens, width = mean_ref.shape
    size = out_ref.shape[0]
    heads = width // HS
    half, at = tokens // 2, heads * size
    pieces = sent_ref[at : at + half, :].astype(jnp.float32)
    lse = pieces + pltpu.roll(pieces, LANES - heads, 1)
    lse = jnp.concatenate([lse, pltpu.roll(lse, LANES // 2, 1)], axis=0)
    matched = sent_ref[at + half : at + half + 1, :].astype(jnp.float32) > 0
    share = 1.0 / (1.0 + jnp.exp(lse_ref[...] - jnp.where(matched, lse, NEG_FILL)))

    def one_group(group, share):
        for inner in range(GROUP):
            head = group * GROUP + inner
            lanes = lanes_of(head)
            part = share[:, inner : inner + 1]
            own = mean_ref[:size, lanes]
            guest = sent_ref[rows_of(head, size), :].astype(jnp.float32)
            out_ref[:, lanes] = (own + part[:size] * (guest - own)).astype(jnp.bfloat16)
            if left_refs:
                later = jnp.broadcast_to(part[size:], (tokens - size, HS))
                own = mean_ref[size:, lanes]
                left_refs[0][:, lanes] = own - later * own
                left_refs[1][:, lanes] = later
        return pltpu.roll(share, LANES - GROUP, 1)

    lax.fori_loop(0, heads // GROUP, one_group, share)


def last_kernel(scaled_ref, share_ref, sent_ref, _, out_ref):
    size, width = scaled_ref.shape
    for head in range(width // HS):
        lanes = slice(head * HS, (head + 1) * HS)
        guest = sent_ref[head * size : (head + 1) * size, :].astype(jnp.float32)
        out_ref[:, lanes] = (scaled_ref[:, lanes] + share_ref[:, lanes] * guest).astype(jnp.bfloat16)


def token_rows(first, size, width):
    return pl.BlockSpec((pl.Element(size), pl.Element(width)), lambda i: (first, 0))


def whole(shape):
    return pl.BlockSpec(shape, lambda i: (0, 0))


def merge(mean, lse, backs, start, sizes, before):
    total, width = mean.shape
    tokens = sum(sizes)
    size, later = sizes[0], sizes[1:]
    left = [jax.ShapeDtypeStruct((later[0], width), jnp.float32)] * 2 if later else []
    result = jax.ShapeDtypeStruct((total, width), jnp.bfloat16)
    params = pltpu.CompilerParams(vmem_limit_bytes=16 * 2**20)
    out, *left = pl.pallas_call(
        merge_kernel,
        grid=(1,),
        in_specs=[
            token_rows(start, tokens, width),
            token_rows(start, tokens, LANES),
            whole(backs[0].shape),
        ]
        + [IN_PLACE] * len(before),
        out_specs=[token_rows(start, size, width)] + [whole(part.shape) for part in left],
        out_shape=[result] + left,
        input_output_aliases={3: 0} if before else {},
        compiler_params=params,
        cost_estimate=pl.CostEstimate(
            flops=4 * tokens * width, bytes_accessed=8 * tokens * width, transcendentals=0
        ),
        name="merge",
    )(mean, lse, backs[0], *before)
    if not later:
        return out
    return pl.pallas_call(
        last_kernel,
        grid=(1,),
        in_specs=[whole(left[0].shape), whole(left[1].shape), whole(backs[1].shape), IN_PLACE],
        out_specs=token_rows(start + size, later[0], width),
        out_shape=result,
        input_output_aliases={3: 0},
        compiler_params=params,
        name="last_merge",
    )(*left, backs[1], out)


def matchings(slots):
    if len(slots) < 2:
        return [[]]
    first, rest = slots[0], slots[1:]
    found = list(matchings(rest))
    for other in rest:
        left = [slot for slot in rest if slot != other]
        found += [[(first, other)] + more for more in matchings(left)]
    return found


def device_pairs(matching, slot_count, slot_devices):
    other = {slot: slot for slot in range(slot_count)}
    for one, two in matching:
        other[one], other[two] = two, one
    pairs = []
    for slot in range(slot_count):
        for inner in range(slot_devices):
            target = inner if other[slot] != slot else inner ^ 1
            pairs.append((slot * slot_devices + inner, other[slot] * slot_devices + target))
    return pairs


def prepare(request_of_slot, query, every):
    width = query.shape[1]
    part = QUERY_ROWS[0] * COLS

    def kernel(request_hbm, query_hbm, number_hbm, part_hbm, request_ref, number_ref, held, sems):
        asked = pltpu.make_async_copy(request_hbm, request_ref, sems.at[0])
        told = pltpu.make_async_copy(number_ref, number_hbm, sems.at[1])
        pieces = [pl.ds(piece * (part // PIECES), part // PIECES) for piece in range(PIECES)]
        takes = [
            pltpu.make_async_copy(query_hbm.at[rows], held.at[rows], sems.at[2 + piece])
            for piece, rows in enumerate(pieces)
        ]
        puts = [
            pltpu.make_async_copy(held.at[rows], part_hbm.at[rows], sems.at[2 + PIECES + piece])
            for piece, rows in enumerate(pieces)
        ]
        asked.start()
        for take in takes:
            take.start()
        asked.wait()
        chosen = jnp.int32(0)
        for number, matching in enumerate(every):
            fits = functools.reduce(
                jnp.logical_and, [request_ref[one] == request_ref[other] for one, other in matching]
            )
            chosen = jnp.where(fits, jnp.int32(number), chosen)
        number_ref[0] = chosen
        told.start()
        for take, put in zip(takes, puts):
            take.wait()
            put.start()
        for put in puts:
            put.wait()
        told.wait()

    number, first_part = pl.pallas_call(
        kernel,
        in_specs=[IN_PLACE] * 2,
        out_specs=[IN_PLACE] * 2,
        out_shape=[
            jax.ShapeDtypeStruct((1,), jnp.int32),
            jax.ShapeDtypeStruct((part, width), query.dtype),
        ],
        scratch_shapes=[
            pltpu.SMEM(request_of_slot.shape, jnp.int32),
            pltpu.SMEM((1,), jnp.int32),
            pltpu.VMEM((part, width), query.dtype),
            pltpu.SemaphoreType.DMA((2 + 2 * PIECES,)),
        ],
        name="prepare",
    )(request_of_slot, query)
    return number[0], first_part


def few_slots(query_vectors, key_vectors, value_vectors, request_of_slot):
    device_count = lax.axis_size("view")
    slot_count = request_of_slot.shape[0]
    slot_devices = device_count // slot_count
    token_count = ROWS * COLS
    width = HEADS * HS
    query = query_vectors.reshape(token_count, width)
    key = key_vectors.reshape(token_count, width)
    value = value_vectors.reshape(token_count, width)
    every = [matching for matching in matchings(list(range(slot_count))) if matching]
    my_slot = lax.axis_index("view") // slot_devices
    branch, first_part = prepare(request_of_slot, query, every)

    def exchange(matching):
        pairs = device_pairs(matching, slot_count, slot_devices)
        members = [slot for pair in matching for slot in pair]

        def run(key, value, query, first_part):
            return pair_attention(key, value, query, first_part)

        def pair_attention(key, value, query, first_part):
            guests = [lax.ppermute(first_part, "view", pairs)]
            start = first_part.shape[0]
            for rows in QUERY_ROWS[1:]:
                sent = lax.slice_in_dim(query, start, start + rows * COLS)
                guests.append(lax.ppermute(sent, "view", pairs))
                start += rows * COLS
            keys = (key, partner(key, "view", 0))
            values = (value, partner(value, "view", 0))
            mean, lse = own_attention(query, keys, values)
            matched = functools.reduce(jnp.logical_or, [my_slot == slot for slot in members])
            matched = matched.astype(jnp.int32).reshape(1)
            returns, start = [], 0
            for guest, rows in zip(guests, RETURN_ROWS):
                sizes = [row * COLS for row in rows]
                sent = guest_attention(matched, guest, keys, values, start, sizes, lse)
                backs = [lax.ppermute(part, "view", pairs) for part in sent]
                returns.append((backs, start, sizes))
                start += guest.shape[0]
            out = ()
            for backs, start, sizes in returns:
                out = (merge(mean, lse, backs, start, sizes, out),)
            return out[0]

        return run

    branches = [exchange(matching) for matching in every]
    attended = lax.switch(branch, branches, key, value, query, first_part)
    return attended.reshape(1, ROWS, COLS, HEADS * HS)


def shards(query_vectors, key_vectors, value_vectors, request_of_slot):
    most_views = request_of_slot.shape[0] // 2
    path = few_slots if most_views == 2 else many_slots
    return path(query_vectors, key_vectors, value_vectors, request_of_slot)


def solution(mesh):
    return jax.shard_map(
        shards,
        mesh=mesh,
        in_specs=(
            P(("groups", "view"), None, None, None),
            P(("groups", "view"), None, None, None),
            P(("groups", "view"), None, None, None),
            P("groups"),
        ),
        out_specs=P(("groups", "view"), None, None, None),
        check_vma=False,
    )
```

```python
import functools

import jax
import jax.numpy as jnp
from jax import lax
from jax.experimental import pallas as pl
from jax.experimental.pallas import tpu as pltpu
from jax.sharding import PartitionSpec as P


HEADS = 32
HS = 128
ROWS = 16
COLS = 8


NEG_FILL = -1e30


def partner(value, axis, distance):
    return lax.ppermute(value, axis, [(i, i ^ 1 << distance) for i in range(lax.axis_size(axis))])


def masked_softmax(scores, allowed):
    scores = jnp.where(allowed, scores, NEG_FILL)
    maximum = jnp.max(scores, axis=-1)
    raised = jnp.exp(scores - maximum[..., None])
    totals = jnp.sum(raised, axis=-1)
    return (maximum, totals, raised.astype(jnp.bfloat16))


def combine(first_part, second_part):
    highest = jnp.maximum(first_part[0], second_part[0])
    first_scale = jnp.exp(first_part[0] - highest)
    second_scale = jnp.exp(second_part[0] - highest)
    denominator = first_part[1] * first_scale + second_part[1] * second_scale
    numerator = first_part[2] * first_scale[..., None] + second_part[2] * second_scale[..., None]
    return (numerator / denominator[..., None]).astype(jnp.bfloat16)


def into_rows(tensor, row_blocks, head_groups):
    trailing = tensor.shape[3:]
    block_rows = tensor.shape[0] // row_blocks
    width_cols = tensor.shape[1]
    group_heads = tensor.shape[2] // head_groups
    shaped = tensor.reshape(
        (row_blocks, block_rows, width_cols, head_groups, group_heads) + trailing
    )
    permuted = (0, 3, 1, 2, 4) + tuple(range(5, 5 + len(trailing)))
    return shaped.transpose(permuted).reshape(
        (row_blocks * head_groups, block_rows, width_cols, group_heads) + trailing
    )


def into_tokens(tensor, row_blocks, head_groups):
    trailing = tensor.shape[4:]
    block_rows = tensor.shape[1]
    width_cols = tensor.shape[2]
    group_heads = tensor.shape[3]
    shaped = tensor.reshape(
        (row_blocks, head_groups, block_rows, width_cols, group_heads) + trailing
    )
    permuted = (0, 2, 3, 1, 4) + tuple(range(5, 5 + len(trailing)))
    return shaped.transpose(permuted).reshape(
        (row_blocks * block_rows * width_cols, head_groups * group_heads) + trailing
    )


def many_slots(query_vectors, key_vectors, value_vectors, request_of_slot):
    scaling = HS ** (-0.5)
    token_count = ROWS * COLS
    partner_key, partner_value = partner((key_vectors, value_vectors), "view", 0)
    head_blocks = 4
    block_heads = HEADS // head_blocks
    own_query = query_vectors.reshape(token_count, head_blocks, block_heads, HS)
    both_keys = jnp.concatenate(
        [
            key_vectors.reshape(token_count, head_blocks, block_heads, HS),
            partner_key.reshape(token_count, head_blocks, block_heads, HS),
        ],
        axis=0,
    )
    both_values = jnp.concatenate(
        [
            value_vectors.reshape(token_count, head_blocks, block_heads, HS),
            partner_value.reshape(token_count, head_blocks, block_heads, HS),
        ],
        axis=0,
    )
    query_row = jnp.arange(token_count) // COLS
    key_row = jnp.arange(2 * token_count) % token_count // COLS
    local_allowed = query_row[:, None] != key_row[None, :]

    def local_block(triple):
        block_scores = (
            jnp.einsum("nhx,khx->hnk", triple[0], triple[1], preferred_element_type=jnp.float32)
            * scaling
        )
        block_peak, block_total, block_weights = masked_softmax(block_scores, local_allowed[None])
        block_sum = jnp.einsum(
            "hnk,khx->nhx", block_weights, triple[2], preferred_element_type=jnp.float32
        )
        return (block_peak.T, block_total.T, block_sum)

    block_peaks, block_totals, block_sums = lax.map(
        local_block,
        (
            jnp.moveaxis(own_query, 1, 0),
            jnp.moveaxis(both_keys, 1, 0),
            jnp.moveaxis(both_values, 1, 0),
        ),
    )
    local_peak = jnp.moveaxis(block_peaks, 0, 1).reshape(token_count, HEADS)
    local_total = jnp.moveaxis(block_totals, 0, 1).reshape(token_count, HEADS)
    local_sum = jnp.moveaxis(block_sums, 0, 1).reshape(token_count, HEADS, HS)
    device_count = lax.axis_size("view")
    slot_count = device_count // 4
    pass_images = device_count // 2
    head_groups = 8
    row_blocks = device_count // head_groups
    block_rows = ROWS // row_blocks
    slot_request = jnp.broadcast_to(
        request_of_slot[:, None], (request_of_slot.shape[0], 2 * COLS)
    ).reshape(-1)
    row_allowed = slot_request[:, None] == slot_request[None, :]

    def arrange(tensor):
        shaped = tensor.reshape(slot_count, 2, 2, block_rows, COLS, HS).transpose(1, 3, 0, 2, 4, 5)
        return shaped.reshape(2 * block_rows, pass_images * COLS, HS)

    def restore(tensor):
        trailing = tensor.shape[2:]
        shaped = tensor.reshape((2, block_rows, slot_count, 2, COLS) + trailing)
        permuted = (2, 0, 3, 1, 4) + tuple(range(5, 5 + len(trailing)))
        return shaped.transpose(permuted).reshape((device_count, block_rows, COLS) + trailing)

    def one_head(triple):
        row_scores = (
            jnp.einsum(
                "bnx,bkx->bnk",
                arrange(triple[0]),
                arrange(triple[1]),
                preferred_element_type=jnp.float32,
            )
            * scaling
        )
        row_peak, row_total, row_weights = masked_softmax(row_scores, row_allowed[None])
        row_sum = jnp.einsum(
            "bnk,bkx->bnx", row_weights, arrange(triple[2]), preferred_element_type=jnp.float32
        )
        return (restore(row_peak), restore(row_total), restore(row_sum))

    query_rows = into_rows(query_vectors.reshape(ROWS, COLS, HEADS, HS), row_blocks, head_groups)
    key_rows = into_rows(key_vectors.reshape(ROWS, COLS, HEADS, HS), row_blocks, head_groups)
    value_rows = into_rows(value_vectors.reshape(ROWS, COLS, HEADS, HS), row_blocks, head_groups)
    by_head = (
        jnp.moveaxis(
            lax.all_to_all(query_rows, "view", split_axis=0, concat_axis=0, tiled=True), 3, 0
        ),
        jnp.moveaxis(
            lax.all_to_all(key_rows, "view", split_axis=0, concat_axis=0, tiled=True), 3, 0
        ),
        jnp.moveaxis(
            lax.all_to_all(value_rows, "view", split_axis=0, concat_axis=0, tiled=True), 3, 0
        ),
    )
    row_peaks, row_totals, row_sums = lax.map(one_head, by_head)
    peak_part = jnp.moveaxis(row_peaks, 0, 3)
    total_part = jnp.moveaxis(row_totals, 0, 3)
    sum_part = jnp.moveaxis(row_sums, 0, 3)
    row_peak = lax.all_to_all(peak_part, "view", split_axis=0, concat_axis=0, tiled=True)
    row_total = lax.all_to_all(total_part, "view", split_axis=0, concat_axis=0, tiled=True)
    row_sum = lax.all_to_all(sum_part, "view", split_axis=0, concat_axis=0, tiled=True)
    row_peak = into_tokens(row_peak, row_blocks, head_groups)
    row_total = into_tokens(row_total, row_blocks, head_groups)
    row_sum = into_tokens(row_sum, row_blocks, head_groups)
    attended = combine((local_peak, local_total, local_sum), (row_peak, row_total, row_sum))
    return attended.reshape(1, ROWS, COLS, HEADS * HS)


SCALING = HS ** (-0.5)
LANES = 128
MARKER = 8
GROUP = 8
QUERY_ROWS = (8, 8)
RETURN_ROWS = ((8,), (6, 2))
IN_VMEM = pl.BlockSpec(memory_space=pltpu.VMEM)
IN_PLACE = pl.BlockSpec(memory_space=pl.ANY)


def scores_of(query, keys):
    return lax.dot_general(query, keys, (((1,), (1,)), ((), ())), preferred_element_type=jnp.float32)


def lanes_of(head):
    return pl.ds(pl.multiple_of(head * HS, HS), HS)


def partial_softmax(heads, query_ref, key_refs, value_refs, rows, allowed):
    scores = []
    for head in heads:
        at = lanes_of(head)
        keys = jnp.concatenate([ref[rows, at] for ref in key_refs], axis=0)
        scores.append(scores_of(query_ref[:, at], keys))
    if allowed is not None:
        scores = [jnp.where(allowed, score, NEG_FILL) for score in scores]
    peaks = [jnp.max(score, axis=1, keepdims=True) for score in scores]
    weights = [
        jnp.exp((score - peak) * SCALING).astype(jnp.bfloat16)
        for score, peak in zip(scores, peaks)
    ]
    results = []
    for head, peak, weight in zip(heads, peaks, weights):
        at = lanes_of(head)
        values = jnp.concatenate([ref[rows, at] for ref in value_refs], axis=0)
        ones = jnp.ones_like(values)
        both = jnp.dot(
            weight, jnp.concatenate([values, ones], axis=1), preferred_element_type=jnp.float32
        )
        total = both[:, HS:]
        results.append((both[:, :HS] / total, peak * SCALING + jnp.log(total)))
    return results


def own_kernel(query_ref, first_key, second_key, first_value, second_value, mean_ref, lse_ref):
    heads = query_ref.shape[1] // HS
    lane = lax.broadcasted_iota(jnp.int32, lse_ref.shape, 1)

    def one_group(group, found):
        numbers = [group * GROUP + inner for inner in range(GROUP)]
        results = partial_softmax(
            numbers, query_ref, (first_key, second_key), (first_value, second_value), slice(None), None
        )
        for head, (mean, lse) in zip(numbers, results):
            mean_ref[:, lanes_of(head)] = mean
            found = jnp.where(lane == head, lse, found)
        return found

    zeros = jnp.zeros(lse_ref.shape, jnp.float32)
    lse_ref[...] = lax.fori_loop(0, heads // GROUP, one_group, zeros)


def own_attention(query, keys, values):
    tokens, width = query.shape
    return pl.pallas_call(
        own_kernel,
        out_shape=[
            jax.ShapeDtypeStruct((tokens, width), jnp.float32),
            jax.ShapeDtypeStruct((tokens, LANES), jnp.float32),
        ],
        compiler_params=pltpu.CompilerParams(vmem_limit_bytes=24 * 2**20),
        cost_estimate=pl.CostEstimate(
            flops=8 * tokens * tokens * width, bytes_accessed=14 * tokens * width, transcendentals=0
        ),
        name="own_attention",
    )(query, *keys, *values)


def rows_of(head, tokens):
    return pl.ds(pl.multiple_of(head * tokens, tokens), tokens)


def guest_kernel(start, matched, query_ref, first_key, second_key, first_value, second_value, _, *sent_refs):
    tokens, width = query_ref.shape
    heads = width // HS
    rows = slice(start, start + tokens)
    shape = (tokens, 2 * tokens)
    query_row = lax.broadcasted_iota(jnp.int32, shape, 0) // COLS
    key_row = lax.broadcasted_iota(jnp.int32, shape, 1) % tokens // COLS
    same_row = query_row == key_row
    lane = lax.broadcasted_iota(jnp.int32, (tokens, LANES), 1)
    firsts = [0]
    for sent_ref in sent_refs[1:]:
        firsts.append(tokens - sent_ref.shape[0] // heads)
    sizes = [stop - first for first, stop in zip(firsts, firsts[1:] + [tokens])]

    def one_group(group, found):
        numbers = [group * GROUP + inner for inner in range(GROUP)]
        results = partial_softmax(
            numbers, query_ref, (first_key, second_key), (first_value, second_value), rows, same_row
        )
        for head, (mean, lse) in zip(numbers, results):
            for sent_ref, first, size in zip(sent_refs, firsts, sizes):
                part = mean[first : first + size].astype(jnp.bfloat16)
                sent_ref[rows_of(head, size), :] = part
            found = jnp.where(lane % heads == head, lse, found)
        return found

    found = lax.fori_loop(0, heads // GROUP, one_group, jnp.zeros((tokens, LANES), jnp.float32))
    high = found.astype(jnp.bfloat16).astype(jnp.float32)
    pieces = jnp.where(lane // heads % 2 == 0, high, found - high)
    half, at = tokens // 2, heads * sizes[0]
    packed = jnp.where(lane[:half] < LANES // 2, pieces[:half], pieces[half:])
    sent_refs[0][at : at + half, :] = packed.astype(jnp.bfloat16)
    marker = jnp.full((MARKER, LANES), matched[0], jnp.int32)
    sent_refs[0][at + half :, :] = marker.astype(jnp.float32).astype(jnp.bfloat16)


def guest_attention(matched, query, keys, values, start, sizes, after):
    tokens, width = query.shape
    heads = width // HS
    lengths = [heads * size for size in sizes]
    lengths[0] += tokens // 2 + MARKER
    return pl.pallas_call(
        functools.partial(guest_kernel, start),
        in_specs=[pl.BlockSpec(memory_space=pltpu.SMEM)] + [IN_VMEM] * 5 + [IN_PLACE],
        out_specs=[IN_VMEM] * len(sizes),
        out_shape=[jax.ShapeDtypeStruct((length, LANES), jnp.bfloat16) for length in lengths],
        compiler_params=pltpu.CompilerParams(vmem_limit_bytes=24 * 2**20),
        cost_estimate=pl.CostEstimate(
            flops=8 * tokens * tokens * width, bytes_accessed=12 * tokens * width, transcendentals=0
        ),
        name="guest_attention",
    )(matched, query, *keys, *values, after)


def merge_kernel(mean_ref, lse_ref, sent_ref, *rest):
    out_ref, left_refs = (rest[-3], rest[-2:]) if len(rest) > 2 else (rest[-1], ())
    tokens, width = mean_ref.shape
    size = out_ref.shape[0]
    heads = width // HS
    half, at = tokens // 2, heads * size
    pieces = sent_ref[at : at + half, :].astype(jnp.float32)
    lse = pieces + pltpu.roll(pieces, LANES - heads, 1)
    lse = jnp.concatenate([lse, pltpu.roll(lse, LANES // 2, 1)], axis=0)
    matched = sent_ref[at + half : at + half + 1, :].astype(jnp.float32) > 0
    share = 1.0 / (1.0 + jnp.exp(lse_ref[...] - jnp.where(matched, lse, NEG_FILL)))

    def one_group(group, share):
        for inner in range(GROUP):
            head = group * GROUP + inner
            lanes = lanes_of(head)
            part = share[:, inner : inner + 1]
            own = mean_ref[:size, lanes]
            guest = sent_ref[rows_of(head, size), :].astype(jnp.float32)
            out_ref[:, lanes] = (own + part[:size] * (guest - own)).astype(jnp.bfloat16)
            if left_refs:
                later = jnp.broadcast_to(part[size:], (tokens - size, HS))
                own = mean_ref[size:, lanes]
                left_refs[0][:, lanes] = own - later * own
                left_refs[1][:, lanes] = later
        return pltpu.roll(share, LANES - GROUP, 1)

    lax.fori_loop(0, heads // GROUP, one_group, share)


def last_kernel(scaled_ref, share_ref, sent_ref, _, out_ref):
    size, width = scaled_ref.shape
    for head in range(width // HS):
        lanes = slice(head * HS, (head + 1) * HS)
        guest = sent_ref[head * size : (head + 1) * size, :].astype(jnp.float32)
        out_ref[:, lanes] = (scaled_ref[:, lanes] + share_ref[:, lanes] * guest).astype(jnp.bfloat16)


def token_rows(first, size, width):
    return pl.BlockSpec((pl.Element(size), pl.Element(width)), lambda i: (first, 0))


def whole(shape):
    return pl.BlockSpec(shape, lambda i: (0, 0))


def merge(mean, lse, backs, start, sizes, before):
    total, width = mean.shape
    tokens = sum(sizes)
    size, later = sizes[0], sizes[1:]
    left = [jax.ShapeDtypeStruct((later[0], width), jnp.float32)] * 2 if later else []
    result = jax.ShapeDtypeStruct((total, width), jnp.bfloat16)
    params = pltpu.CompilerParams(vmem_limit_bytes=16 * 2**20)
    out, *left = pl.pallas_call(
        merge_kernel,
        grid=(1,),
        in_specs=[
            token_rows(start, tokens, width),
            token_rows(start, tokens, LANES),
            whole(backs[0].shape),
        ]
        + [IN_PLACE] * len(before),
        out_specs=[token_rows(start, size, width)] + [whole(part.shape) for part in left],
        out_shape=[result] + left,
        input_output_aliases={3: 0} if before else {},
        compiler_params=params,
        cost_estimate=pl.CostEstimate(
            flops=4 * tokens * width, bytes_accessed=8 * tokens * width, transcendentals=0
        ),
        name="merge",
    )(mean, lse, backs[0], *before)
    if not later:
        return out
    return pl.pallas_call(
        last_kernel,
        grid=(1,),
        in_specs=[whole(left[0].shape), whole(left[1].shape), whole(backs[1].shape), IN_PLACE],
        out_specs=token_rows(start + size, later[0], width),
        out_shape=result,
        input_output_aliases={3: 0},
        compiler_params=params,
        name="last_merge",
    )(*left, backs[1], out)


def matchings(slots):
    if len(slots) < 2:
        return [[]]
    first, rest = slots[0], slots[1:]
    found = list(matchings(rest))
    for other in rest:
        left = [slot for slot in rest if slot != other]
        found += [[(first, other)] + more for more in matchings(left)]
    return found


def device_pairs(matching, slot_count, slot_devices):
    other = {slot: slot for slot in range(slot_count)}
    for one, two in matching:
        other[one], other[two] = two, one
    pairs = []
    for slot in range(slot_count):
        for inner in range(slot_devices):
            target = inner if other[slot] != slot else inner ^ 1
            pairs.append((slot * slot_devices + inner, other[slot] * slot_devices + target))
    return pairs


def prepare(request_of_slot, query, every):
    slot_count, width = request_of_slot.shape[0], query.shape[1]
    part = QUERY_ROWS[0] * COLS
    slot_devices = lax.axis_size("view") // slot_count

    def kernel(request_hbm, query_hbm, number_hbm, matched_hbm, part_ref, request_ref, numbers, matched, sems):
        asked = pltpu.make_async_copy(request_hbm, request_ref, sems.at[0])
        taken = pltpu.make_async_copy(query_hbm.at[pl.ds(0, part)], part_ref, sems.at[1])
        told = pltpu.make_async_copy(numbers, number_hbm, sems.at[2])
        noted = pltpu.make_async_copy(matched, matched_hbm, sems.at[3])
        asked.start()
        taken.start()
        my_slot = lax.axis_index("view") // slot_devices
        asked.wait()
        chosen = jnp.int32(0)
        for number, matching in enumerate(every):
            fits = functools.reduce(
                jnp.logical_and, [request_ref[one] == request_ref[other] for one, other in matching]
            )
            chosen = jnp.where(fits, jnp.int32(number), chosen)
        numbers[0] = chosen
        told.start()
        mine = request_ref[my_slot]
        sharing = [(request_ref[slot] == mine).astype(jnp.int32) for slot in range(slot_count)]
        matched[0] = sum(sharing) - 1
        noted.start()
        taken.wait()
        told.wait()
        noted.wait()

    number, matched, first_part = pl.pallas_call(
        kernel,
        in_specs=[IN_PLACE] * 2,
        out_specs=[IN_PLACE, IN_PLACE, IN_VMEM],
        out_shape=[
            jax.ShapeDtypeStruct((1,), jnp.int32),
            jax.ShapeDtypeStruct((1,), jnp.int32),
            jax.ShapeDtypeStruct((part, width), query.dtype),
        ],
        scratch_shapes=[
            pltpu.SMEM(request_of_slot.shape, jnp.int32),
            pltpu.SMEM((1,), jnp.int32),
            pltpu.SMEM((1,), jnp.int32),
            pltpu.SemaphoreType.DMA((4,)),
        ],
        name="prepare",
    )(request_of_slot, query)
    return number[0], matched, first_part


def few_slots(query_vectors, key_vectors, value_vectors, request_of_slot):
    device_count = lax.axis_size("view")
    slot_count = request_of_slot.shape[0]
    slot_devices = device_count // slot_count
    token_count = ROWS * COLS
    width = HEADS * HS
    query = query_vectors.reshape(token_count, width)
    key = key_vectors.reshape(token_count, width)
    value = value_vectors.reshape(token_count, width)
    every = [matching for matching in matchings(list(range(slot_count))) if matching]
    branch, matched, first_part = prepare(request_of_slot, query, every)

    def exchange(matching):
        pairs = device_pairs(matching, slot_count, slot_devices)

        def run(key, value, query, first_part, matched):
            return pair_attention(key, value, query, first_part, matched)

        def pair_attention(key, value, query, first_part, matched):
            guests = [lax.ppermute(first_part, "view", pairs)]
            start = first_part.shape[0]
            for rows in QUERY_ROWS[1:]:
                sent = lax.slice_in_dim(query, start, start + rows * COLS)
                guests.append(lax.ppermute(sent, "view", pairs))
                start += rows * COLS
            keys = (key, partner(key, "view", 0))
            values = (value, partner(value, "view", 0))
            mean, lse = own_attention(query, keys, values)
            returns, start = [], 0
            for guest, rows in zip(guests, RETURN_ROWS):
                sizes = [row * COLS for row in rows]
                sent = guest_attention(matched, guest, keys, values, start, sizes, lse)
                backs = [lax.ppermute(part, "view", pairs) for part in sent]
                returns.append((backs, start, sizes))
                start += guest.shape[0]
            out = ()
            for backs, start, sizes in returns:
                out = (merge(mean, lse, backs, start, sizes, out),)
            return out[0]

        return run

    branches = [exchange(matching) for matching in every]
    attended = lax.switch(branch, branches, key, value, query, first_part, matched)
    return attended.reshape(1, ROWS, COLS, HEADS * HS)


def shards(query_vectors, key_vectors, value_vectors, request_of_slot):
    most_views = request_of_slot.shape[0] // 2
    path = few_slots if most_views == 2 else many_slots
    return path(query_vectors, key_vectors, value_vectors, request_of_slot)


def solution(mesh):
    return jax.shard_map(
        shards,
        mesh=mesh,
        in_specs=(
            P(("groups", "view"), None, None, None),
            P(("groups", "view"), None, None, None),
            P(("groups", "view"), None, None, None),
            P("groups"),
        ),
        out_specs=P(("groups", "view"), None, None, None),
        check_vma=False,
    )
```

```python
import functools

import jax
import jax.numpy as jnp
from jax import lax
from jax.experimental import pallas as pl
from jax.experimental.pallas import tpu as pltpu
from jax.sharding import PartitionSpec as P


HEADS = 32
HS = 128
ROWS = 16
COLS = 8


NEG_FILL = -1e30


def partner(value, axis, distance):
    return lax.ppermute(value, axis, [(i, i ^ 1 << distance) for i in range(lax.axis_size(axis))])


def masked_softmax(scores, allowed):
    scores = jnp.where(allowed, scores, NEG_FILL)
    maximum = jnp.max(scores, axis=-1)
    raised = jnp.exp(scores - maximum[..., None])
    totals = jnp.sum(raised, axis=-1)
    return (maximum, totals, raised.astype(jnp.bfloat16))


def combine(first_part, second_part):
    highest = jnp.maximum(first_part[0], second_part[0])
    first_scale = jnp.exp(first_part[0] - highest)
    second_scale = jnp.exp(second_part[0] - highest)
    denominator = first_part[1] * first_scale + second_part[1] * second_scale
    numerator = first_part[2] * first_scale[..., None] + second_part[2] * second_scale[..., None]
    return (numerator / denominator[..., None]).astype(jnp.bfloat16)


def into_rows(tensor, row_blocks, head_groups):
    trailing = tensor.shape[3:]
    block_rows = tensor.shape[0] // row_blocks
    width_cols = tensor.shape[1]
    group_heads = tensor.shape[2] // head_groups
    shaped = tensor.reshape(
        (row_blocks, block_rows, width_cols, head_groups, group_heads) + trailing
    )
    permuted = (0, 3, 1, 2, 4) + tuple(range(5, 5 + len(trailing)))
    return shaped.transpose(permuted).reshape(
        (row_blocks * head_groups, block_rows, width_cols, group_heads) + trailing
    )


def into_tokens(tensor, row_blocks, head_groups):
    trailing = tensor.shape[4:]
    block_rows = tensor.shape[1]
    width_cols = tensor.shape[2]
    group_heads = tensor.shape[3]
    shaped = tensor.reshape(
        (row_blocks, head_groups, block_rows, width_cols, group_heads) + trailing
    )
    permuted = (0, 2, 3, 1, 4) + tuple(range(5, 5 + len(trailing)))
    return shaped.transpose(permuted).reshape(
        (row_blocks * block_rows * width_cols, head_groups * group_heads) + trailing
    )


def many_slots(query_vectors, key_vectors, value_vectors, request_of_slot):
    scaling = HS ** (-0.5)
    token_count = ROWS * COLS
    partner_key, partner_value = partner((key_vectors, value_vectors), "view", 0)
    head_blocks = 4
    block_heads = HEADS // head_blocks
    own_query = query_vectors.reshape(token_count, head_blocks, block_heads, HS)
    both_keys = jnp.concatenate(
        [
            key_vectors.reshape(token_count, head_blocks, block_heads, HS),
            partner_key.reshape(token_count, head_blocks, block_heads, HS),
        ],
        axis=0,
    )
    both_values = jnp.concatenate(
        [
            value_vectors.reshape(token_count, head_blocks, block_heads, HS),
            partner_value.reshape(token_count, head_blocks, block_heads, HS),
        ],
        axis=0,
    )
    query_row = jnp.arange(token_count) // COLS
    key_row = jnp.arange(2 * token_count) % token_count // COLS
    local_allowed = query_row[:, None] != key_row[None, :]

    def local_block(triple):
        block_scores = (
            jnp.einsum("nhx,khx->hnk", triple[0], triple[1], preferred_element_type=jnp.float32)
            * scaling
        )
        block_peak, block_total, block_weights = masked_softmax(block_scores, local_allowed[None])
        block_sum = jnp.einsum(
            "hnk,khx->nhx", block_weights, triple[2], preferred_element_type=jnp.float32
        )
        return (block_peak.T, block_total.T, block_sum)

    block_peaks, block_totals, block_sums = lax.map(
        local_block,
        (
            jnp.moveaxis(own_query, 1, 0),
            jnp.moveaxis(both_keys, 1, 0),
            jnp.moveaxis(both_values, 1, 0),
        ),
    )
    local_peak = jnp.moveaxis(block_peaks, 0, 1).reshape(token_count, HEADS)
    local_total = jnp.moveaxis(block_totals, 0, 1).reshape(token_count, HEADS)
    local_sum = jnp.moveaxis(block_sums, 0, 1).reshape(token_count, HEADS, HS)
    device_count = lax.axis_size("view")
    slot_count = device_count // 4
    pass_images = device_count // 2
    head_groups = 8
    row_blocks = device_count // head_groups
    block_rows = ROWS // row_blocks
    slot_request = jnp.broadcast_to(
        request_of_slot[:, None], (request_of_slot.shape[0], 2 * COLS)
    ).reshape(-1)
    row_allowed = slot_request[:, None] == slot_request[None, :]

    def arrange(tensor):
        shaped = tensor.reshape(slot_count, 2, 2, block_rows, COLS, HS).transpose(1, 3, 0, 2, 4, 5)
        return shaped.reshape(2 * block_rows, pass_images * COLS, HS)

    def restore(tensor):
        trailing = tensor.shape[2:]
        shaped = tensor.reshape((2, block_rows, slot_count, 2, COLS) + trailing)
        permuted = (2, 0, 3, 1, 4) + tuple(range(5, 5 + len(trailing)))
        return shaped.transpose(permuted).reshape((device_count, block_rows, COLS) + trailing)

    def one_head(triple):
        row_scores = (
            jnp.einsum(
                "bnx,bkx->bnk",
                arrange(triple[0]),
                arrange(triple[1]),
                preferred_element_type=jnp.float32,
            )
            * scaling
        )
        row_peak, row_total, row_weights = masked_softmax(row_scores, row_allowed[None])
        row_sum = jnp.einsum(
            "bnk,bkx->bnx", row_weights, arrange(triple[2]), preferred_element_type=jnp.float32
        )
        return (restore(row_peak), restore(row_total), restore(row_sum))

    query_rows = into_rows(query_vectors.reshape(ROWS, COLS, HEADS, HS), row_blocks, head_groups)
    key_rows = into_rows(key_vectors.reshape(ROWS, COLS, HEADS, HS), row_blocks, head_groups)
    value_rows = into_rows(value_vectors.reshape(ROWS, COLS, HEADS, HS), row_blocks, head_groups)
    by_head = (
        jnp.moveaxis(
            lax.all_to_all(query_rows, "view", split_axis=0, concat_axis=0, tiled=True), 3, 0
        ),
        jnp.moveaxis(
            lax.all_to_all(key_rows, "view", split_axis=0, concat_axis=0, tiled=True), 3, 0
        ),
        jnp.moveaxis(
            lax.all_to_all(value_rows, "view", split_axis=0, concat_axis=0, tiled=True), 3, 0
        ),
    )
    row_peaks, row_totals, row_sums = lax.map(one_head, by_head)
    peak_part = jnp.moveaxis(row_peaks, 0, 3)
    total_part = jnp.moveaxis(row_totals, 0, 3)
    sum_part = jnp.moveaxis(row_sums, 0, 3)
    row_peak = lax.all_to_all(peak_part, "view", split_axis=0, concat_axis=0, tiled=True)
    row_total = lax.all_to_all(total_part, "view", split_axis=0, concat_axis=0, tiled=True)
    row_sum = lax.all_to_all(sum_part, "view", split_axis=0, concat_axis=0, tiled=True)
    row_peak = into_tokens(row_peak, row_blocks, head_groups)
    row_total = into_tokens(row_total, row_blocks, head_groups)
    row_sum = into_tokens(row_sum, row_blocks, head_groups)
    attended = combine((local_peak, local_total, local_sum), (row_peak, row_total, row_sum))
    return attended.reshape(1, ROWS, COLS, HEADS * HS)


SCALING = HS ** (-0.5)
LANES = 128
GROUP = 8
QUERY_ROWS = (8, 8)
RETURN_ROWS = ((8,), (6, 2))
IN_VMEM = pl.BlockSpec(memory_space=pltpu.VMEM)
IN_PLACE = pl.BlockSpec(memory_space=pl.ANY)


def scores_of(query, keys):
    return lax.dot_general(query, keys, (((1,), (1,)), ((), ())), preferred_element_type=jnp.float32)


def lanes_of(head):
    return pl.ds(pl.multiple_of(head * HS, HS), HS)


def partial_softmax(heads, query_ref, key_refs, value_refs, rows, allowed):
    scores = []
    for head in heads:
        at = lanes_of(head)
        keys = jnp.concatenate([ref[rows, at] for ref in key_refs], axis=0)
        scores.append(scores_of(query_ref[:, at], keys))
    if allowed is not None:
        scores = [jnp.where(allowed, score, NEG_FILL) for score in scores]
    peaks = [jnp.max(score, axis=1, keepdims=True) for score in scores]
    weights = [
        jnp.exp((score - peak) * SCALING).astype(jnp.bfloat16)
        for score, peak in zip(scores, peaks)
    ]
    results = []
    for head, peak, weight in zip(heads, peaks, weights):
        at = lanes_of(head)
        values = jnp.concatenate([ref[rows, at] for ref in value_refs], axis=0)
        ones = jnp.ones_like(values)
        both = jnp.dot(
            weight, jnp.concatenate([values, ones], axis=1), preferred_element_type=jnp.float32
        )
        total = both[:, HS:]
        results.append((both[:, :HS] / total, peak * SCALING + jnp.log(total)))
    return results


def own_kernel(query_ref, first_key, second_key, first_value, second_value, mean_ref, lse_ref):
    heads = query_ref.shape[1] // HS
    lane = lax.broadcasted_iota(jnp.int32, lse_ref.shape, 1)

    def one_group(group, found):
        numbers = [group * GROUP + inner for inner in range(GROUP)]
        results = partial_softmax(
            numbers, query_ref, (first_key, second_key), (first_value, second_value), slice(None), None
        )
        for head, (mean, lse) in zip(numbers, results):
            mean_ref[:, lanes_of(head)] = mean
            found = jnp.where(lane == head, lse, found)
        return found

    zeros = jnp.zeros(lse_ref.shape, jnp.float32)
    lse_ref[...] = lax.fori_loop(0, heads // GROUP, one_group, zeros)


def own_attention(query, keys, values):
    tokens, width = query.shape
    return pl.pallas_call(
        own_kernel,
        out_shape=[
            jax.ShapeDtypeStruct((tokens, width), jnp.float32),
            jax.ShapeDtypeStruct((tokens, LANES), jnp.float32),
        ],
        compiler_params=pltpu.CompilerParams(vmem_limit_bytes=24 * 2**20),
        cost_estimate=pl.CostEstimate(
            flops=8 * tokens * tokens * width, bytes_accessed=14 * tokens * width, transcendentals=0
        ),
        name="own_attention",
    )(query, *keys, *values)


def rows_of(head, tokens):
    return pl.ds(pl.multiple_of(head * tokens, tokens), tokens)


def guest_kernel(start, matched, query_ref, first_key, second_key, first_value, second_value, _, *sent_refs):
    tokens, width = query_ref.shape
    heads = width // HS
    rows = slice(start, start + tokens)
    shape = (tokens, 2 * tokens)
    query_row = lax.broadcasted_iota(jnp.int32, shape, 0) // COLS
    key_row = lax.broadcasted_iota(jnp.int32, shape, 1) % tokens // COLS
    same_row = query_row == key_row
    lane = lax.broadcasted_iota(jnp.int32, (tokens, LANES), 1)
    firsts = [0]
    for sent_ref in sent_refs[1:]:
        firsts.append(tokens - sent_ref.shape[0] // heads)
    sizes = [stop - first for first, stop in zip(firsts, firsts[1:] + [tokens])]

    def one_group(group, found):
        numbers = [group * GROUP + inner for inner in range(GROUP)]
        results = partial_softmax(
            numbers, query_ref, (first_key, second_key), (first_value, second_value), rows, same_row
        )
        for head, (mean, lse) in zip(numbers, results):
            for sent_ref, first, size in zip(sent_refs, firsts, sizes):
                part = mean[first : first + size].astype(jnp.bfloat16)
                sent_ref[rows_of(head, size), :] = part
            found = jnp.where(lane % heads == head, lse, found)
        return found

    found = lax.fori_loop(0, heads // GROUP, one_group, jnp.zeros((tokens, LANES), jnp.float32))
    found = jnp.where(jnp.full(found.shape, matched[0], jnp.int32) > 0, found, NEG_FILL)
    high = found.astype(jnp.bfloat16).astype(jnp.float32)
    pieces = jnp.where(lane // heads % 2 == 0, high, found - high)
    half, at = tokens // 2, heads * sizes[0]
    packed = jnp.where(lane[:half] < LANES // 2, pieces[:half], pieces[half:])
    sent_refs[0][at : at + half, :] = packed.astype(jnp.bfloat16)


def guest_attention(matched, query, keys, values, start, sizes, after):
    tokens, width = query.shape
    heads = width // HS
    lengths = [heads * size for size in sizes]
    lengths[0] += tokens // 2
    return pl.pallas_call(
        functools.partial(guest_kernel, start),
        in_specs=[pl.BlockSpec(memory_space=pltpu.SMEM)] + [IN_VMEM] * 5 + [IN_PLACE],
        out_specs=[IN_VMEM] * len(sizes),
        out_shape=[jax.ShapeDtypeStruct((length, LANES), jnp.bfloat16) for length in lengths],
        compiler_params=pltpu.CompilerParams(vmem_limit_bytes=24 * 2**20),
        cost_estimate=pl.CostEstimate(
            flops=8 * tokens * tokens * width, bytes_accessed=12 * tokens * width, transcendentals=0
        ),
        name="guest_attention",
    )(matched, query, *keys, *values, after)


def merge_kernel(mean_ref, lse_ref, sent_ref, *rest):
    out_ref, left_refs = (rest[-3], rest[-2:]) if len(rest) > 2 else (rest[-1], ())
    tokens, width = mean_ref.shape
    size = out_ref.shape[0]
    heads = width // HS
    half, at = tokens // 2, heads * size
    pieces = sent_ref[at : at + half, :].astype(jnp.float32)
    lse = pieces + pltpu.roll(pieces, LANES - heads, 1)
    lse = jnp.concatenate([lse, pltpu.roll(lse, LANES // 2, 1)], axis=0)
    share = 1.0 / (1.0 + jnp.exp(lse_ref[...] - lse))

    def one_group(group, share):
        for inner in range(GROUP):
            head = group * GROUP + inner
            lanes = lanes_of(head)
            part = share[:, inner : inner + 1]
            own = mean_ref[:size, lanes]
            guest = sent_ref[rows_of(head, size), :].astype(jnp.float32)
            out_ref[:, lanes] = (own + part[:size] * (guest - own)).astype(jnp.bfloat16)
            if left_refs:
                later = jnp.broadcast_to(part[size:], (tokens - size, HS))
                own = mean_ref[size:, lanes]
                left_refs[0][:, lanes] = own - later * own
                left_refs[1][:, lanes] = later
        return pltpu.roll(share, LANES - GROUP, 1)

    lax.fori_loop(0, heads // GROUP, one_group, share)


def last_kernel(scaled_ref, share_ref, sent_ref, _, out_ref):
    size, width = scaled_ref.shape
    for head in range(width // HS):
        lanes = slice(head * HS, (head + 1) * HS)
        guest = sent_ref[head * size : (head + 1) * size, :].astype(jnp.float32)
        out_ref[:, lanes] = (scaled_ref[:, lanes] + share_ref[:, lanes] * guest).astype(jnp.bfloat16)


def token_rows(first, size, width):
    return pl.BlockSpec((pl.Element(size), pl.Element(width)), lambda i: (first, 0))


def whole(shape):
    return pl.BlockSpec(shape, lambda i: (0, 0))


def merge(mean, lse, backs, start, sizes, before):
    total, width = mean.shape
    tokens = sum(sizes)
    size, later = sizes[0], sizes[1:]
    left = [jax.ShapeDtypeStruct((later[0], width), jnp.float32)] * 2 if later else []
    result = jax.ShapeDtypeStruct((total, width), jnp.bfloat16)
    params = pltpu.CompilerParams(vmem_limit_bytes=16 * 2**20)
    out, *left = pl.pallas_call(
        merge_kernel,
        grid=(1,),
        in_specs=[
            token_rows(start, tokens, width),
            token_rows(start, tokens, LANES),
            whole(backs[0].shape),
        ]
        + [IN_PLACE] * len(before),
        out_specs=[token_rows(start, size, width)] + [whole(part.shape) for part in left],
        out_shape=[result] + left,
        input_output_aliases={3: 0} if before else {},
        compiler_params=params,
        cost_estimate=pl.CostEstimate(
            flops=4 * tokens * width, bytes_accessed=8 * tokens * width, transcendentals=0
        ),
        name="merge",
    )(mean, lse, backs[0], *before)
    if not later:
        return out
    return pl.pallas_call(
        last_kernel,
        grid=(1,),
        in_specs=[whole(left[0].shape), whole(left[1].shape), whole(backs[1].shape), IN_PLACE],
        out_specs=token_rows(start + size, later[0], width),
        out_shape=result,
        input_output_aliases={3: 0},
        compiler_params=params,
        name="last_merge",
    )(*left, backs[1], out)


def matchings(slots):
    if len(slots) < 2:
        return [[]]
    first, rest = slots[0], slots[1:]
    found = list(matchings(rest))
    for other in rest:
        left = [slot for slot in rest if slot != other]
        found += [[(first, other)] + more for more in matchings(left)]
    return found


def device_pairs(matching, slot_count, slot_devices):
    other = {slot: slot for slot in range(slot_count)}
    for one, two in matching:
        other[one], other[two] = two, one
    pairs = []
    for slot in range(slot_count):
        for inner in range(slot_devices):
            target = inner if other[slot] != slot else inner ^ 1
            pairs.append((slot * slot_devices + inner, other[slot] * slot_devices + target))
    return pairs


def prepare(request_of_slot, query, every):
    slot_count, width = request_of_slot.shape[0], query.shape[1]
    part = QUERY_ROWS[0] * COLS
    slot_devices = lax.axis_size("view") // slot_count

    def kernel(request_hbm, query_hbm, number_hbm, matched_hbm, part_ref, request_ref, numbers, matched, sems):
        asked = pltpu.make_async_copy(request_hbm, request_ref, sems.at[0])
        taken = pltpu.make_async_copy(query_hbm.at[pl.ds(0, part)], part_ref, sems.at[1])
        told = pltpu.make_async_copy(numbers, number_hbm, sems.at[2])
        noted = pltpu.make_async_copy(matched, matched_hbm, sems.at[3])
        asked.start()
        taken.start()
        my_slot = lax.axis_index("view") // slot_devices
        asked.wait()
        chosen = jnp.int32(0)
        for number, matching in enumerate(every):
            fits = functools.reduce(
                jnp.logical_and, [request_ref[one] == request_ref[other] for one, other in matching]
            )
            chosen = jnp.where(fits, jnp.int32(number), chosen)
        numbers[0] = chosen
        told.start()
        mine = request_ref[my_slot]
        sharing = [(request_ref[slot] == mine).astype(jnp.int32) for slot in range(slot_count)]
        matched[0] = sum(sharing) - 1
        noted.start()
        taken.wait()
        told.wait()
        noted.wait()

    number, matched, first_part = pl.pallas_call(
        kernel,
        in_specs=[IN_PLACE] * 2,
        out_specs=[IN_PLACE, IN_PLACE, IN_VMEM],
        out_shape=[
            jax.ShapeDtypeStruct((1,), jnp.int32),
            jax.ShapeDtypeStruct((1,), jnp.int32),
            jax.ShapeDtypeStruct((part, width), query.dtype),
        ],
        scratch_shapes=[
            pltpu.SMEM(request_of_slot.shape, jnp.int32),
            pltpu.SMEM((1,), jnp.int32),
            pltpu.SMEM((1,), jnp.int32),
            pltpu.SemaphoreType.DMA((4,)),
        ],
        name="prepare",
    )(request_of_slot, query)
    return number[0], matched, first_part


def few_slots(query_vectors, key_vectors, value_vectors, request_of_slot):
    device_count = lax.axis_size("view")
    slot_count = request_of_slot.shape[0]
    slot_devices = device_count // slot_count
    token_count = ROWS * COLS
    width = HEADS * HS
    query = query_vectors.reshape(token_count, width)
    key = key_vectors.reshape(token_count, width)
    value = value_vectors.reshape(token_count, width)
    every = [matching for matching in matchings(list(range(slot_count))) if matching]
    half = slot_count // 2
    every.sort(key=lambda pairs: (len(pairs), sum(abs(two - one - half) for one, two in pairs)))
    branch, matched, first_part = prepare(request_of_slot, query, every)

    def exchange(matching):
        pairs = device_pairs(matching, slot_count, slot_devices)

        def run(key, value, query, first_part, matched):
            return pair_attention(key, value, query, first_part, matched)

        def pair_attention(key, value, query, first_part, matched):
            guests = [lax.ppermute(first_part, "view", pairs)]
            start = first_part.shape[0]
            for rows in QUERY_ROWS[1:]:
                sent = lax.slice_in_dim(query, start, start + rows * COLS)
                guests.append(lax.ppermute(sent, "view", pairs))
                start += rows * COLS
            keys = (key, partner(key, "view", 0))
            values = (value, partner(value, "view", 0))
            mean, lse = own_attention(query, keys, values)
            returns, start = [], 0
            for guest, rows in zip(guests, RETURN_ROWS):
                sizes = [row * COLS for row in rows]
                sent = guest_attention(matched, guest, keys, values, start, sizes, lse)
                backs = [lax.ppermute(part, "view", pairs) for part in sent]
                returns.append((backs, start, sizes))
                start += guest.shape[0]
            out = ()
            for backs, start, sizes in returns:
                out = (merge(mean, lse, backs, start, sizes, out),)
            return out[0]

        return run

    branches = [exchange(matching) for matching in every]
    attended = lax.switch(branch, branches, key, value, query, first_part, matched)
    return attended.reshape(1, ROWS, COLS, HEADS * HS)


def shards(query_vectors, key_vectors, value_vectors, request_of_slot):
    most_views = request_of_slot.shape[0] // 2
    path = few_slots if most_views == 2 else many_slots
    return path(query_vectors, key_vectors, value_vectors, request_of_slot)


def solution(mesh):
    return jax.shard_map(
        shards,
        mesh=mesh,
        in_specs=(
            P(("groups", "view"), None, None, None),
            P(("groups", "view"), None, None, None),
            P(("groups", "view"), None, None, None),
            P("groups"),
        ),
        out_specs=P(("groups", "view"), None, None, None),
        check_vma=False,
    )
```

```python
import functools

import jax
import jax.numpy as jnp
from jax import lax
from jax.experimental import pallas as pl
from jax.experimental.pallas import tpu as pltpu
from jax.sharding import PartitionSpec as P


HEADS = 32
HS = 128
ROWS = 16
COLS = 8


NEG_FILL = -1e30


def partner(value, axis, distance):
    return lax.ppermute(value, axis, [(i, i ^ 1 << distance) for i in range(lax.axis_size(axis))])


def masked_softmax(scores, allowed):
    scores = jnp.where(allowed, scores, NEG_FILL)
    maximum = jnp.max(scores, axis=-1)
    raised = jnp.exp(scores - maximum[..., None])
    totals = jnp.sum(raised, axis=-1)
    return (maximum, totals, raised.astype(jnp.bfloat16))


def combine(first_part, second_part):
    highest = jnp.maximum(first_part[0], second_part[0])
    first_scale = jnp.exp(first_part[0] - highest)
    second_scale = jnp.exp(second_part[0] - highest)
    denominator = first_part[1] * first_scale + second_part[1] * second_scale
    numerator = first_part[2] * first_scale[..., None] + second_part[2] * second_scale[..., None]
    return (numerator / denominator[..., None]).astype(jnp.bfloat16)


def into_rows(tensor, row_blocks, head_groups):
    trailing = tensor.shape[3:]
    block_rows = tensor.shape[0] // row_blocks
    width_cols = tensor.shape[1]
    group_heads = tensor.shape[2] // head_groups
    shaped = tensor.reshape(
        (row_blocks, block_rows, width_cols, head_groups, group_heads) + trailing
    )
    permuted = (0, 3, 1, 2, 4) + tuple(range(5, 5 + len(trailing)))
    return shaped.transpose(permuted).reshape(
        (row_blocks * head_groups, block_rows, width_cols, group_heads) + trailing
    )


def into_tokens(tensor, row_blocks, head_groups):
    trailing = tensor.shape[4:]
    block_rows = tensor.shape[1]
    width_cols = tensor.shape[2]
    group_heads = tensor.shape[3]
    shaped = tensor.reshape(
        (row_blocks, head_groups, block_rows, width_cols, group_heads) + trailing
    )
    permuted = (0, 2, 3, 1, 4) + tuple(range(5, 5 + len(trailing)))
    return shaped.transpose(permuted).reshape(
        (row_blocks * block_rows * width_cols, head_groups * group_heads) + trailing
    )


def many_slots(query_vectors, key_vectors, value_vectors, request_of_slot):
    scaling = HS ** (-0.5)
    token_count = ROWS * COLS
    partner_key, partner_value = partner((key_vectors, value_vectors), "view", 0)
    head_blocks = 4
    block_heads = HEADS // head_blocks
    own_query = query_vectors.reshape(token_count, head_blocks, block_heads, HS)
    both_keys = jnp.concatenate(
        [
            key_vectors.reshape(token_count, head_blocks, block_heads, HS),
            partner_key.reshape(token_count, head_blocks, block_heads, HS),
        ],
        axis=0,
    )
    both_values = jnp.concatenate(
        [
            value_vectors.reshape(token_count, head_blocks, block_heads, HS),
            partner_value.reshape(token_count, head_blocks, block_heads, HS),
        ],
        axis=0,
    )
    query_row = jnp.arange(token_count) // COLS
    key_row = jnp.arange(2 * token_count) % token_count // COLS
    local_allowed = query_row[:, None] != key_row[None, :]

    def local_block(triple):
        block_scores = (
            jnp.einsum("nhx,khx->hnk", triple[0], triple[1], preferred_element_type=jnp.float32)
            * scaling
        )
        block_peak, block_total, block_weights = masked_softmax(block_scores, local_allowed[None])
        block_sum = jnp.einsum(
            "hnk,khx->nhx", block_weights, triple[2], preferred_element_type=jnp.float32
        )
        return (block_peak.T, block_total.T, block_sum)

    block_peaks, block_totals, block_sums = lax.map(
        local_block,
        (
            jnp.moveaxis(own_query, 1, 0),
            jnp.moveaxis(both_keys, 1, 0),
            jnp.moveaxis(both_values, 1, 0),
        ),
    )
    local_peak = jnp.moveaxis(block_peaks, 0, 1).reshape(token_count, HEADS)
    local_total = jnp.moveaxis(block_totals, 0, 1).reshape(token_count, HEADS)
    local_sum = jnp.moveaxis(block_sums, 0, 1).reshape(token_count, HEADS, HS)
    device_count = lax.axis_size("view")
    slot_count = device_count // 4
    pass_images = device_count // 2
    head_groups = 8
    row_blocks = device_count // head_groups
    block_rows = ROWS // row_blocks
    slot_request = jnp.broadcast_to(
        request_of_slot[:, None], (request_of_slot.shape[0], 2 * COLS)
    ).reshape(-1)
    row_allowed = slot_request[:, None] == slot_request[None, :]

    def arrange(tensor):
        shaped = tensor.reshape(slot_count, 2, 2, block_rows, COLS, HS).transpose(1, 3, 0, 2, 4, 5)
        return shaped.reshape(2 * block_rows, pass_images * COLS, HS)

    def restore(tensor):
        trailing = tensor.shape[2:]
        shaped = tensor.reshape((2, block_rows, slot_count, 2, COLS) + trailing)
        permuted = (2, 0, 3, 1, 4) + tuple(range(5, 5 + len(trailing)))
        return shaped.transpose(permuted).reshape((device_count, block_rows, COLS) + trailing)

    def one_head(triple):
        row_scores = (
            jnp.einsum(
                "bnx,bkx->bnk",
                arrange(triple[0]),
                arrange(triple[1]),
                preferred_element_type=jnp.float32,
            )
            * scaling
        )
        row_peak, row_total, row_weights = masked_softmax(row_scores, row_allowed[None])
        row_sum = jnp.einsum(
            "bnk,bkx->bnx", row_weights, arrange(triple[2]), preferred_element_type=jnp.float32
        )
        return (restore(row_peak), restore(row_total), restore(row_sum))

    query_rows = into_rows(query_vectors.reshape(ROWS, COLS, HEADS, HS), row_blocks, head_groups)
    key_rows = into_rows(key_vectors.reshape(ROWS, COLS, HEADS, HS), row_blocks, head_groups)
    value_rows = into_rows(value_vectors.reshape(ROWS, COLS, HEADS, HS), row_blocks, head_groups)
    by_head = (
        jnp.moveaxis(
            lax.all_to_all(query_rows, "view", split_axis=0, concat_axis=0, tiled=True), 3, 0
        ),
        jnp.moveaxis(
            lax.all_to_all(key_rows, "view", split_axis=0, concat_axis=0, tiled=True), 3, 0
        ),
        jnp.moveaxis(
            lax.all_to_all(value_rows, "view", split_axis=0, concat_axis=0, tiled=True), 3, 0
        ),
    )
    row_peaks, row_totals, row_sums = lax.map(one_head, by_head)
    peak_part = jnp.moveaxis(row_peaks, 0, 3)
    total_part = jnp.moveaxis(row_totals, 0, 3)
    sum_part = jnp.moveaxis(row_sums, 0, 3)
    row_peak = lax.all_to_all(peak_part, "view", split_axis=0, concat_axis=0, tiled=True)
    row_total = lax.all_to_all(total_part, "view", split_axis=0, concat_axis=0, tiled=True)
    row_sum = lax.all_to_all(sum_part, "view", split_axis=0, concat_axis=0, tiled=True)
    row_peak = into_tokens(row_peak, row_blocks, head_groups)
    row_total = into_tokens(row_total, row_blocks, head_groups)
    row_sum = into_tokens(row_sum, row_blocks, head_groups)
    attended = combine((local_peak, local_total, local_sum), (row_peak, row_total, row_sum))
    return attended.reshape(1, ROWS, COLS, HEADS * HS)


SCALING = HS ** (-0.5)
LANES = 128
GROUP = 8
QUERY_ROWS = (8, 8)
RETURN_ROWS = ((8,), (6, 2))
IN_VMEM = pl.BlockSpec(memory_space=pltpu.VMEM)
IN_PLACE = pl.BlockSpec(memory_space=pl.ANY)


def scores_of(query, keys):
    return lax.dot_general(query, keys, (((1,), (1,)), ((), ())), preferred_element_type=jnp.float32)


def lanes_of(head):
    return pl.ds(pl.multiple_of(head * HS, HS), HS)


def partial_softmax(heads, query_ref, key_refs, value_refs, rows, allowed):
    scores = []
    for head in heads:
        at = lanes_of(head)
        keys = jnp.concatenate([ref[rows, at] for ref in key_refs], axis=0)
        scores.append(scores_of(query_ref[:, at], keys))
    if allowed is not None:
        scores = [jnp.where(allowed, score, NEG_FILL) for score in scores]
    peaks = [jnp.max(score, axis=1, keepdims=True) for score in scores]
    weights = [
        jnp.exp((score - peak) * SCALING).astype(jnp.bfloat16)
        for score, peak in zip(scores, peaks)
    ]
    results = []
    for head, peak, weight in zip(heads, peaks, weights):
        at = lanes_of(head)
        values = jnp.concatenate([ref[rows, at] for ref in value_refs], axis=0)
        ones = jnp.ones_like(values)
        both = jnp.dot(
            weight, jnp.concatenate([values, ones], axis=1), preferred_element_type=jnp.float32
        )
        total = both[:, HS:]
        results.append((both[:, :HS] / total, peak * SCALING + jnp.log(total)))
    return results


def own_kernel(query_ref, first_key, second_key, first_value, second_value, mean_ref, lse_ref):
    heads = query_ref.shape[1] // HS
    lane = lax.broadcasted_iota(jnp.int32, lse_ref.shape, 1)

    def one_group(group, found):
        numbers = [group * GROUP + inner for inner in range(GROUP)]
        results = partial_softmax(
            numbers, query_ref, (first_key, second_key), (first_value, second_value), slice(None), None
        )
        for head, (mean, lse) in zip(numbers, results):
            mean_ref[:, lanes_of(head)] = mean
            found = jnp.where(lane == head, lse, found)
        return found

    zeros = jnp.zeros(lse_ref.shape, jnp.float32)
    lse_ref[...] = lax.fori_loop(0, heads // GROUP, one_group, zeros)


def own_attention(query, keys, values):
    tokens, width = query.shape
    return pl.pallas_call(
        own_kernel,
        out_shape=[
            jax.ShapeDtypeStruct((tokens, width), jnp.float32),
            jax.ShapeDtypeStruct((tokens, LANES), jnp.float32),
        ],
        compiler_params=pltpu.CompilerParams(vmem_limit_bytes=24 * 2**20),
        cost_estimate=pl.CostEstimate(
            flops=8 * tokens * tokens * width, bytes_accessed=14 * tokens * width, transcendentals=0
        ),
        name="own_attention",
    )(query, *keys, *values)


def rows_of(head, tokens):
    return pl.ds(pl.multiple_of(head * tokens, tokens), tokens)


def guest_kernel(start, members, slot_devices, query_ref, first_key, second_key, first_value, second_value, _, *sent_refs):
    tokens, width = query_ref.shape
    heads = width // HS
    rows = slice(start, start + tokens)
    shape = (tokens, 2 * tokens)
    query_row = lax.broadcasted_iota(jnp.int32, shape, 0) // COLS
    key_row = lax.broadcasted_iota(jnp.int32, shape, 1) % tokens // COLS
    same_row = query_row == key_row
    lane = lax.broadcasted_iota(jnp.int32, (tokens, LANES), 1)
    firsts = [0]
    for sent_ref in sent_refs[1:]:
        firsts.append(tokens - sent_ref.shape[0] // heads)
    sizes = [stop - first for first, stop in zip(firsts, firsts[1:] + [tokens])]

    def one_group(group, found):
        numbers = [group * GROUP + inner for inner in range(GROUP)]
        results = partial_softmax(
            numbers, query_ref, (first_key, second_key), (first_value, second_value), rows, same_row
        )
        for head, (mean, lse) in zip(numbers, results):
            for sent_ref, first, size in zip(sent_refs, firsts, sizes):
                part = mean[first : first + size].astype(jnp.bfloat16)
                sent_ref[rows_of(head, size), :] = part
            found = jnp.where(lane % heads == head, lse, found)
        return found

    found = lax.fori_loop(0, heads // GROUP, one_group, jnp.zeros((tokens, LANES), jnp.float32))
    my_slot = jnp.full(found.shape, lax.axis_index("view") // slot_devices, jnp.int32)
    matched = functools.reduce(jnp.logical_or, [my_slot == slot for slot in members])
    found = jnp.where(matched, found, NEG_FILL)
    high = found.astype(jnp.bfloat16).astype(jnp.float32)
    pieces = jnp.where(lane // heads % 2 == 0, high, found - high)
    half, at = tokens // 2, heads * sizes[0]
    packed = jnp.where(lane[:half] < LANES // 2, pieces[:half], pieces[half:])
    sent_refs[0][at : at + half, :] = packed.astype(jnp.bfloat16)


def guest_attention(query, keys, values, start, sizes, members, slot_devices, after):
    tokens, width = query.shape
    heads = width // HS
    lengths = [heads * size for size in sizes]
    lengths[0] += tokens // 2
    return pl.pallas_call(
        functools.partial(guest_kernel, start, members, slot_devices),
        in_specs=[IN_VMEM] * 5 + [IN_PLACE],
        out_specs=[IN_VMEM] * len(sizes),
        out_shape=[jax.ShapeDtypeStruct((length, LANES), jnp.bfloat16) for length in lengths],
        compiler_params=pltpu.CompilerParams(vmem_limit_bytes=24 * 2**20),
        cost_estimate=pl.CostEstimate(
            flops=8 * tokens * tokens * width, bytes_accessed=12 * tokens * width, transcendentals=0
        ),
        name="guest_attention",
    )(query, *keys, *values, after)


def merge_kernel(mean_ref, lse_ref, sent_ref, *rest):
    out_ref, left_refs = (rest[-3], rest[-2:]) if len(rest) > 2 else (rest[-1], ())
    tokens, width = mean_ref.shape
    size = out_ref.shape[0]
    heads = width // HS
    half, at = tokens // 2, heads * size
    pieces = sent_ref[at : at + half, :].astype(jnp.float32)
    lse = pieces + pltpu.roll(pieces, LANES - heads, 1)
    lse = jnp.concatenate([lse, pltpu.roll(lse, LANES // 2, 1)], axis=0)
    share = 1.0 / (1.0 + jnp.exp(lse_ref[...] - lse))

    def one_group(group, share):
        for inner in range(GROUP):
            head = group * GROUP + inner
            lanes = lanes_of(head)
            part = share[:, inner : inner + 1]
            own = mean_ref[:size, lanes]
            guest = sent_ref[rows_of(head, size), :].astype(jnp.float32)
            out_ref[:, lanes] = (own + part[:size] * (guest - own)).astype(jnp.bfloat16)
            if left_refs:
                later = jnp.broadcast_to(part[size:], (tokens - size, HS))
                own = mean_ref[size:, lanes]
                left_refs[0][:, lanes] = own - later * own
                left_refs[1][:, lanes] = later
        return pltpu.roll(share, LANES - GROUP, 1)

    lax.fori_loop(0, heads // GROUP, one_group, share)


def last_kernel(scaled_ref, share_ref, sent_ref, _, out_ref):
    size, width = scaled_ref.shape
    for head in range(width // HS):
        lanes = slice(head * HS, (head + 1) * HS)
        guest = sent_ref[head * size : (head + 1) * size, :].astype(jnp.float32)
        out_ref[:, lanes] = (scaled_ref[:, lanes] + share_ref[:, lanes] * guest).astype(jnp.bfloat16)


def token_rows(first, size, width):
    return pl.BlockSpec((pl.Element(size), pl.Element(width)), lambda i: (first, 0))


def whole(shape):
    return pl.BlockSpec(shape, lambda i: (0, 0))


def merge(mean, lse, backs, start, sizes, before):
    total, width = mean.shape
    tokens = sum(sizes)
    size, later = sizes[0], sizes[1:]
    left = [jax.ShapeDtypeStruct((later[0], width), jnp.float32)] * 2 if later else []
    result = jax.ShapeDtypeStruct((total, width), jnp.bfloat16)
    params = pltpu.CompilerParams(vmem_limit_bytes=16 * 2**20)
    out, *left = pl.pallas_call(
        merge_kernel,
        grid=(1,),
        in_specs=[
            token_rows(start, tokens, width),
            token_rows(start, tokens, LANES),
            whole(backs[0].shape),
        ]
        + [IN_PLACE] * len(before),
        out_specs=[token_rows(start, size, width)] + [whole(part.shape) for part in left],
        out_shape=[result] + left,
        input_output_aliases={3: 0} if before else {},
        compiler_params=params,
        cost_estimate=pl.CostEstimate(
            flops=4 * tokens * width, bytes_accessed=8 * tokens * width, transcendentals=0
        ),
        name="merge",
    )(mean, lse, backs[0], *before)
    if not later:
        return out
    return pl.pallas_call(
        last_kernel,
        grid=(1,),
        in_specs=[whole(left[0].shape), whole(left[1].shape), whole(backs[1].shape), IN_PLACE],
        out_specs=token_rows(start + size, later[0], width),
        out_shape=result,
        input_output_aliases={3: 0},
        compiler_params=params,
        name="last_merge",
    )(*left, backs[1], out)


def matchings(slots):
    if len(slots) < 2:
        return [[]]
    first, rest = slots[0], slots[1:]
    found = list(matchings(rest))
    for other in rest:
        left = [slot for slot in rest if slot != other]
        found += [[(first, other)] + more for more in matchings(left)]
    return found


def device_pairs(matching, slot_count, slot_devices):
    other = {slot: slot for slot in range(slot_count)}
    for one, two in matching:
        other[one], other[two] = two, one
    pairs = []
    for slot in range(slot_count):
        for inner in range(slot_devices):
            target = inner if other[slot] != slot else inner ^ 1
            pairs.append((slot * slot_devices + inner, other[slot] * slot_devices + target))
    return pairs


def prepare(request_of_slot, query, every):
    width = query.shape[1]
    part = QUERY_ROWS[0] * COLS

    def kernel(request_hbm, query_hbm, number_hbm, part_ref, request_ref, number_ref, sems):
        asked = pltpu.make_async_copy(request_hbm, request_ref, sems.at[0])
        taken = pltpu.make_async_copy(query_hbm.at[pl.ds(0, part)], part_ref, sems.at[1])
        told = pltpu.make_async_copy(number_ref, number_hbm, sems.at[2])
        asked.start()
        taken.start()
        asked.wait()
        chosen = jnp.int32(0)
        for number, matching in enumerate(every):
            fits = functools.reduce(
                jnp.logical_and, [request_ref[one] == request_ref[other] for one, other in matching]
            )
            chosen = jnp.where(fits, jnp.int32(number), chosen)
        number_ref[0] = chosen
        told.start()
        taken.wait()
        told.wait()

    number, first_part = pl.pallas_call(
        kernel,
        in_specs=[IN_PLACE] * 2,
        out_specs=[IN_PLACE, IN_VMEM],
        out_shape=[
            jax.ShapeDtypeStruct((1,), jnp.int32),
            jax.ShapeDtypeStruct((part, width), query.dtype),
        ],
        scratch_shapes=[
            pltpu.SMEM(request_of_slot.shape, jnp.int32),
            pltpu.SMEM((1,), jnp.int32),
            pltpu.SemaphoreType.DMA((3,)),
        ],
        name="prepare",
    )(request_of_slot, query)
    return number[0], first_part


def few_slots(query_vectors, key_vectors, value_vectors, request_of_slot):
    device_count = lax.axis_size("view")
    slot_count = request_of_slot.shape[0]
    slot_devices = device_count // slot_count
    token_count = ROWS * COLS
    width = HEADS * HS
    query = query_vectors.reshape(token_count, width)
    key = key_vectors.reshape(token_count, width)
    value = value_vectors.reshape(token_count, width)
    every = [matching for matching in matchings(list(range(slot_count))) if matching]
    half = slot_count // 2
    every.sort(key=lambda pairs: (len(pairs), sum(abs(two - one - half) for one, two in pairs)))
    branch, first_part = prepare(request_of_slot, query, every)

    def exchange(matching):
        pairs = device_pairs(matching, slot_count, slot_devices)
        members = [slot for pair in matching for slot in pair]

        def run(key, value, query, first_part):
            return pair_attention(key, value, query, first_part)

        def pair_attention(key, value, query, first_part):
            guests = [lax.ppermute(first_part, "view", pairs)]
            start = first_part.shape[0]
            for rows in QUERY_ROWS[1:]:
                sent = lax.slice_in_dim(query, start, start + rows * COLS)
                guests.append(lax.ppermute(sent, "view", pairs))
                start += rows * COLS
            keys = (key, partner(key, "view", 0))
            values = (value, partner(value, "view", 0))
            mean, lse = own_attention(query, keys, values)
            returns, start = [], 0
            for guest, rows in zip(guests, RETURN_ROWS):
                sizes = [row * COLS for row in rows]
                sent = guest_attention(guest, keys, values, start, sizes, members, slot_devices, lse)
                backs = [lax.ppermute(part, "view", pairs) for part in sent]
                returns.append((backs, start, sizes))
                start += guest.shape[0]
            out = ()
            for backs, start, sizes in returns:
                out = (merge(mean, lse, backs, start, sizes, out),)
            return out[0]

        return run

    branches = [exchange(matching) for matching in every]
    attended = lax.switch(branch, branches, key, value, query, first_part)
    return attended.reshape(1, ROWS, COLS, HEADS * HS)


def shards(query_vectors, key_vectors, value_vectors, request_of_slot):
    most_views = request_of_slot.shape[0] // 2
    path = few_slots if most_views == 2 else many_slots
    return path(query_vectors, key_vectors, value_vectors, request_of_slot)


def solution(mesh):
    return jax.shard_map(
        shards,
        mesh=mesh,
        in_specs=(
            P(("groups", "view"), None, None, None),
            P(("groups", "view"), None, None, None),
            P(("groups", "view"), None, None, None),
            P("groups"),
        ),
        out_specs=P(("groups", "view"), None, None, None),
        check_vma=False,
    )
```
